512 devices in a mesh: seq: 64 (over y_lo, z, core), kv: 8 (over x, y_hi).
Axes of the slice: x: 4, y: 4 (y_hi: 2, y_lo: 2; y = y_hi * 2 + y_lo), z: 16, core: 2. Of those that a mesh axis runs over, the one named last changes fastest.
Arguments:
- queries: bfloat16 [64, 16384, 128], P('kv', 'seq'), may hold values from -56 to 56
- key_states: bfloat16 [8, 16384, 128], P('kv', 'seq'), may hold values from -56 to 56
- samples: int32 [64, 512], P('kv', 'seq'), may hold values from 0 to 16383, as said below
- query_gate_weight: float32 [128, 128], replicated, may hold values from -6 to 6
- key_gate_weight: float32 [384, 128], replicated, may hold values from -0.3125 to 0.3125
Outputs:
- row_loss: float32 [64, 512], P('kv', 'seq')
- query_grad: float32 [128, 128], replicated
- key_grad: float32 [384, 128], replicated
The draws below stay inside these ranges and needn't reach their ends.
Inputs may be any that keep to these rules, and one draw needn't show every extreme that they name: `samples`: sampled row r of every head lies in the tokens r // 8 * 256 to (r // 8 + 1) * 256 - 1; positions may repeat.
All inputs are finite; a program needn't handle non-finite values.
Results may differ from the reference program's by a relative error of at most 0.0003.
Values may be sent and summed in bfloat16 or wider, within the bound.
A program may use at most 64 MiB of HBM per device.

```python
import math
import jax
import jax.numpy as jnp
from jax import lax

D = 128
QPK = 8
GATE = 128
BLOCK = 128
TOK_DEV = 256
ROWS_DEV = 8
KV_HEADS = 8
HEADS = 64
SEQ = 16384
ROWS = 512
NB = 128


def draw_queries(key, part):
    shape_all = (HEADS, SEQ, D)
    entries = jnp.clip(jax.random.normal(jax.random.fold_in(key, 1), shape_all, jnp.float32), -6.0, 6.0)
    return entries.astype(jnp.bfloat16)


def draw_key_states(key, part):
    shape_all = (KV_HEADS, SEQ, D)
    entries = jnp.clip(jax.random.normal(jax.random.fold_in(key, 2), shape_all, jnp.float32), -6.0, 6.0)
    return entries.astype(jnp.bfloat16)


def draw_samples(key, part):
    shard_start = jnp.arange(ROWS, dtype=jnp.int32) // ROWS_DEV * TOK_DEV
    within = jax.random.randint(jax.random.fold_in(key, 5), (HEADS, ROWS), 0, TOK_DEV, dtype=jnp.int32)
    return shard_start[None, :] + within


def centred(key, dims, width, reach, kind=jnp.bfloat16):
    result = jax.random.normal(key, dims, jnp.float32) * width
    return jnp.minimum(jnp.maximum(result, -reach), reach).astype(kind)


def setup_inputs(seed: int = 0) -> dict:
    key_of = jax.random.split(jax.random.key(seed), 6)
    queries = draw_queries(jax.random.fold_in(key_of[5], 71), 0)
    key_states = draw_key_states(jax.random.fold_in(key_of[5], 71), 0)
    samples = draw_samples(jax.random.fold_in(key_of[5], 71), 0)
    query_gate_weight = centred(key_of[3], (D, GATE), 1.0, 6.0, jnp.float32)
    key_gate_weight = centred(key_of[4], (3 * D, GATE), (3 * D) ** -0.5, 0.3125, jnp.float32)
    return {"queries": queries, "key_states": key_states, "samples": samples, "query_gate_weight": query_gate_weight, "key_gate_weight": key_gate_weight}


masked_score = -1e+30
highest = lax.Precision.HIGHEST

def reference(queries, key_states, samples, query_gate_weight, key_gate_weight):
    pooled_query = lax.optimization_barrier(jnp.mean(queries.reshape(HEADS, NB, BLOCK, D), axis=2, dtype=jnp.float32))
    key_blocks = key_states.reshape(KV_HEADS, NB, BLOCK, D)
    pooled_key = jnp.concatenate([lax.optimization_barrier(jnp.max(key_blocks, axis=2)).astype(jnp.float32), lax.optimization_barrier(jnp.min(key_blocks, axis=2)).astype(jnp.float32), lax.optimization_barrier(jnp.mean(key_blocks, axis=2, dtype=jnp.float32))], axis=-1)
    gate_query = jnp.einsum('hcd,dg->hcg', pooled_query, query_gate_weight, precision=highest)
    gate_key = jnp.einsum('kcd,dg->kcg', pooled_key, key_gate_weight, precision=highest)
    key_places = jnp.arange(SEQ, dtype=jnp.int32)
    block_ids = jnp.arange(NB, dtype=jnp.int32)
    score_scale = 1.0 / math.sqrt(D)
    gate_scale = 1.0 / math.sqrt(GATE)

    def one_head(head_index):
        group_index = head_index // QPK
        places = samples[head_index]
        query_rows = queries[head_index][places]
        scores = lax.dot_general(query_rows, key_states[group_index], (((1,), (1,)), ((), ())), preferred_element_type=jnp.float32) * score_scale
        causal = key_places[None, :] <= places[:, None]
        row_top = lax.optimization_barrier(jnp.max(jnp.where(causal, scores, masked_score), axis=1))
        weights = jnp.where(causal, jnp.exp(scores - row_top[:, None]), 0.0)
        block_mass = lax.optimization_barrier(jnp.sum(weights.reshape(ROWS, NB, BLOCK), axis=2))
        teacher = block_mass / lax.optimization_barrier(jnp.sum(block_mass, axis=1, keepdims=True))
        own_block = places // BLOCK
        gate_rows = gate_query[head_index][own_block]
        head_keys = gate_key[group_index]
        logits = jnp.dot(gate_rows, head_keys.T, precision=highest) * gate_scale
        allowed = block_ids[None, :] <= own_block[:, None]
        logit_top = lax.optimization_barrier(jnp.max(jnp.where(allowed, logits, masked_score), axis=1))
        gate_weights = jnp.where(allowed, jnp.exp(logits - logit_top[:, None]), 0.0)
        gate_total = lax.optimization_barrier(jnp.sum(gate_weights, axis=1))
        log_total = logit_top + jnp.log(gate_total)
        row_losses = log_total - lax.optimization_barrier(jnp.sum(jnp.where(allowed, teacher * logits, 0.0), axis=1))
        gate_delta = jnp.where(allowed, gate_weights / gate_total[:, None] - teacher, 0.0)
        query_part = jnp.dot(pooled_query[head_index][own_block].T, jnp.dot(gate_delta, head_keys, precision=highest) * gate_scale, precision=highest)
        key_delta = jnp.dot(gate_delta.T, gate_rows, precision=highest) * gate_scale
        key_part = jnp.dot(pooled_key[group_index].T, key_delta, precision=highest)
        return (row_losses, query_part, key_part)
    losses, query_parts, key_parts = lax.map(one_head, jnp.arange(HEADS, dtype=jnp.int32))
    return (losses, lax.optimization_barrier(jnp.sum(query_parts, axis=0)), lax.optimization_barrier(jnp.sum(key_parts, axis=0)))
```

```python
import functools
import math

import jax
import jax.numpy as jnp
from jax import lax
from jax.experimental import pallas as pl
from jax.experimental.pallas import tpu as pltpu
from jax.sharding import Mesh
from jax.sharding import PartitionSpec as P

BLOCK = 128
PIECES = 4
MESH = pl.DeviceIdType.MESH
LOW = -1e30
highest = lax.Precision.HIGHEST
NN = (((1,), (0,)), ((), ()))
NT = (((1,), (1,)), ((), ()))
TN = (((0,), (0,)), ((), ()))


def dot32(a, b, dims=NN):
    return lax.dot_general(a, b, dims, precision=highest, preferred_element_type=jnp.float32)


def partner(place, apart, size):
    if apart == 0:
        return place
    if size == 2:
        return 1 - place
    return (place + 1 - 2 * (place % 2), (place + 2) % 4, 3 - place)[apart - 1]


def kernel(
    sizes,
    q_ref,
    k_ref,
    samples_ref,
    wq_ref,
    wk_ref,
    loss_ref,
    query_grad_ref,
    key_grad_ref,
    keys,
    pooled,
    queries,
    top,
    mass,
    packed,
    returned,
    part,
    from_core,
    chip_sum,
    from_x,
    x_sum,
    from_y,
    y_sum,
    from_z,
    z_sum,
    y_all,
    x_all,
    whole,
    key_send,
    key_recv,
    pool_send,
    pool_recv,
    slice_send,
    slice_recv,
    sum_send,
    sum_recv,
    z_send,
    z_recv,
):
    nz, nx, nyh = sizes
    ny = 2 * nyh
    half = nz // 2
    z, yl, c = lax.axis_index("z"), lax.axis_index("yl"), lax.axis_index("c")
    x, yh = lax.axis_index("x"), lax.axis_index("yh")
    y = 2 * yh + yl
    started = []

    def send(src, dst, send_sem, recv_sem, target):
        copy = pltpu.make_async_remote_copy(
            src_ref=src,
            dst_ref=dst,
            send_sem=send_sem,
            recv_sem=recv_sem,
            device_id=target,
            device_id_type=MESH,
        )
        copy.start()
        started.append(copy)
        return copy

    def along_z(step):
        return {"z": (z + step + nz) % nz}

    def in_slice(i):
        return {"yl": partner(yl, i // 2, 2), "c": partner(c, i % 2, 2)}

    def along_x(i):
        return {"x": partner(x, i, nx)}

    def along_y(i):
        other = partner(y, i, ny)
        return {"yh": other // 2, "yl": other % 2}

    near = [along_z(1)] + ([along_z(-1)] if nz > 2 else [])
    near += [in_slice(i) for i in (1, 2, 3)]
    near += [along_x(i) for i in range(1, nx)]
    near += [along_y(i) for i in range(2, ny)]
    barrier = pltpu.get_barrier_semaphore()
    for target in near:
        pl.semaphore_signal(barrier, inc=1, device_id=target, device_id_type=MESH)

    own = k_ref[0].astype(jnp.float32)
    blocks = (own[:BLOCK], own[BLOCK:])
    pooled[0, 0] = jnp.concatenate(
        [jnp.max(b, axis=0, keepdims=True) for b in blocks]
        + [jnp.min(b, axis=0, keepdims=True) for b in blocks]
        + [jnp.sum(b, axis=0, keepdims=True) * (1.0 / BLOCK) for b in blocks]
        + [jnp.zeros((2, own.shape[1]), jnp.float32)],
        axis=0,
    )

    pl.semaphore_wait(barrier, len(near))

    rows_piece = k_ref.shape[1] // PIECES
    ways = ((0, 1, half), (1, -1, nz - 1 - half))

    def slot(way, step):
        return step if way == 0 else (nz - step) % nz

    def pass_keys(way, step, piece):
        rows = pl.ds(piece * rows_piece, rows_piece)
        src = k_ref.at[0, rows] if step == 0 else keys.at[slot(way, step), rows]
        return send(
            src,
            keys.at[slot(way, step + 1), rows],
            key_send.at[way, step, piece],
            key_recv.at[way, step, piece],
            along_z(ways[way][1]),
        )

    def pass_pooled(way, step):
        return send(
            pooled.at[slot(way, step)],
            pooled.at[slot(way, step + 1)],
            pool_send.at[way, step],
            pool_recv.at[way, step],
            along_z(ways[way][1]),
        )

    key_copies, pool_copies = {}, {}
    for piece in range(PIECES):
        for way, _, reach in ways:
            if reach:
                key_copies[way, 0, piece] = pass_keys(way, 0, piece)
    pooled_here = [
        send(
            pooled.at[0, 0],
            pooled.at[0, i],
            slice_send.at[0, i - 1],
            slice_recv.at[0, i - 1],
            in_slice(i),
        )
        for i in (1, 2, 3)
    ]

    shard = (yl * nz + z) * 2 + c
    local = (samples_ref[...] - shard * (2 * BLOCK)).astype(jnp.float32)
    spread = jnp.concatenate([jnp.broadcast_to(local[h : h + 1], (8, 8)) for h in range(8)], axis=0)
    lanes8 = lax.broadcasted_iota(jnp.int32, (64, 8), 1)
    rows8 = lax.broadcasted_iota(jnp.int32, (64, 8), 0) % 8
    column = jnp.sum(jnp.where(lanes8 == rows8, spread, 0.0), axis=1, keepdims=True)
    tokens = lax.broadcasted_iota(jnp.int32, (8, 2 * BLOCK), 1)
    query_rows, pooled_rows = [], []
    for h in range(8):
        place = column[8 * h : 8 * h + 8].astype(jnp.int32)
        chosen = jnp.where(tokens == place, 1.0, 0.0)
        block = jnp.where(tokens // BLOCK == place // BLOCK, 1.0, 0.0)
        both = lax.dot_general(
            jnp.concatenate([chosen, block], axis=0).astype(jnp.bfloat16),
            q_ref[h],
            NN,
            preferred_element_type=jnp.float32,
        )
        query_rows.append(both[:8])
        pooled_rows.append(both[8:] * (1.0 / BLOCK))
    queries[0] = jnp.concatenate(query_rows, axis=0).astype(jnp.bfloat16)
    queries_here = [
        send(
            queries.at[0],
            queries.at[i],
            slice_send.at[1, i - 1],
            slice_recv.at[1, i - 1],
            in_slice(i),
        )
        for i in (1, 2, 3)
    ]
    pooled_rows = jnp.concatenate(pooled_rows + [jnp.zeros((64, BLOCK), jnp.float32)], axis=0)
    gate_rows = dot32(pooled_rows, wq_ref[...])
    lanes = lax.broadcasted_iota(jnp.int32, (1, 256), 1)
    eye = lax.broadcasted_iota(jnp.int32, (64, 256), 0) == lax.broadcasted_iota(
        jnp.int32, (64, 256), 1
    )
    places = jnp.sum(jnp.where(eye, column, 0.0), axis=0, keepdims=True).astype(jnp.int32)
    places = jnp.where(lanes < 64, places, 2 * BLOCK - 1)

    for copy in queries_here:
        copy.wait_recv()
    every_query = queries[...].reshape(256, BLOCK)
    exponent = math.log2(math.e) / math.sqrt(BLOCK)

    def score(place):
        block_keys = k_ref[0] if place == 0 else keys[place]
        scores = lax.dot_general(block_keys, every_query, NT, preferred_element_type=jnp.float32)
        if place == 0:
            token = lax.broadcasted_iota(jnp.int32, scores.shape, 0)
            scores = jnp.where(token <= places, scores, LOW)
        for b in range(2):
            part_scores = scores[b * BLOCK : (b + 1) * BLOCK]
            highest_score = jnp.max(part_scores, axis=0, keepdims=True)
            weights = jnp.exp2((part_scores - highest_score) * exponent)
            at = b * nz + place
            top[at : at + 1] = highest_score
            mass[at : at + 1] = jnp.sum(weights, axis=0, keepdims=True)

    score(0)
    for step in range(1, half + 1):
        for piece in range(PIECES):
            for way, _, reach in ways:
                if step <= reach:
                    key_copies[way, step - 1, piece].wait_recv()
                    if step < reach:
                        key_copies[way, step, piece] = pass_keys(way, step, piece)
        if step == 1:
            for copy in pooled_here:
                copy.wait_recv()
        for way, _, reach in ways:
            if 1 < step <= reach + 1:
                pool_copies[way, step - 2].wait_recv()
            if step <= reach:
                pool_copies[way, step - 1] = pass_pooled(way, step - 1)
        for way, _, reach in ways:
            if step <= reach:
                score(slot(way, step))

    first = lax.broadcasted_iota(jnp.int32, (2 * nz, BLOCK), 1) < 64
    for pair in range(2):
        tops = top[:, pair * BLOCK : (pair + 1) * BLOCK]
        masses = mass[:, pair * BLOCK : (pair + 1) * BLOCK]
        packed[2 * pair] = jnp.where(first, tops, pltpu.roll(masses, 64, 1))
        packed[2 * pair + 1] = jnp.where(first, pltpu.roll(tops, 64, 1), masses)
    returns = [
        send(
            packed.at[i],
            returned.at[i],
            slice_send.at[2, i - 1],
            slice_recv.at[2, i - 1],
            in_slice(i),
        )
        for i in (1, 2, 3)
    ]
    for way, _, reach in ways:
        if reach == half:
            pool_copies[way, reach - 1].wait_recv()

    nb = 8 * nz
    pooled_keys = jnp.concatenate(
        [
            jnp.concatenate(
                [
                    pooled[:, i, 2 * kind + b : 2 * kind + b + 1, :].reshape(nz, BLOCK)
                    for kind in range(3)
                ],
                axis=1,
            )
            for i in range(4)
            for b in range(2)
        ],
        axis=0,
    )
    gate_key = dot32(pooled_keys, wk_ref[...])
    gate_scale = 1.0 / math.sqrt(BLOCK)
    logits = dot32(gate_key, gate_rows, NT) * gate_scale
    order = lax.broadcasted_iota(jnp.int32, (nb, BLOCK), 0)
    lane = lax.broadcasted_iota(jnp.int32, (nb, BLOCK), 1)
    i_of = order // (2 * nz)
    b_of = order // nz % 2
    z_of = (z - order % nz + nz) % nz
    yl_of = (yl + i_of // 2) % 2
    c_of = (c + i_of % 2) % 2
    block_of = ((yl_of * nz + z_of) * 2 + c_of) * 2 + b_of
    own_block = 2 * shard + places[:, :BLOCK] // BLOCK
    allowed = block_of <= own_block
    logit_top = jnp.max(jnp.where(allowed, logits, LOW), axis=0, keepdims=True)
    gate_weights = jnp.where(allowed, jnp.exp(logits - logit_top), 0.0)
    gate_total = jnp.sum(gate_weights, axis=0, keepdims=True)
    log_total = logit_top + jnp.log(gate_total)
    gate = gate_weights / gate_total

    for copy in returns:
        copy.wait_recv()
    pairs = jnp.concatenate([packed[0]] + [returned[i] for i in (1, 2, 3)], axis=0)
    sums = pltpu.roll(pairs, 64, 1)
    row_top = jnp.max(jnp.where(allowed, pairs, LOW), axis=0, keepdims=True)
    masses = jnp.where(allowed, sums * jnp.exp2((pairs - row_top) * exponent), 0.0)
    teacher = masses / jnp.sum(masses, axis=0, keepdims=True)
    losses = log_total - jnp.sum(jnp.where(allowed, teacher * logits, 0.0), axis=0, keepdims=True)
    delta = jnp.where(allowed & (lane < 64), (gate - teacher) * gate_scale, 0.0)

    head_of = lax.broadcasted_iota(jnp.int32, (8, BLOCK), 1) // 8
    head = lax.broadcasted_iota(jnp.int32, (8, BLOCK), 0)
    row_of = lax.broadcasted_iota(jnp.int32, (BLOCK, BLOCK), 0) % 8
    row = lax.broadcasted_iota(jnp.int32, (BLOCK, BLOCK), 1)

    block_query = dot32(delta, pooled_rows)
    local_sum = dot32(block_query, pooled_keys, TN)
    part[0] = local_sum[:, :256]
    part[1, :, :BLOCK] = local_sum[:, 256:]
    part[1, :, BLOCK:] = jnp.zeros((BLOCK, BLOCK), jnp.float32)
    other_core = {"c": 1 - c}
    copy = send(part.at[1 - c], from_core, sum_send.at[0], sum_recv.at[0], other_core)
    by_head = jnp.where(head_of == head, jnp.broadcast_to(losses, (8, BLOCK)), 0.0)
    loss_ref[...] = dot32(by_head, jnp.where(row_of == row, 1.0, 0.0))[:, :8]
    copy.wait_recv()
    chip_sum[...] = part[c] + from_core[...]

    rows_x = BLOCK // nx
    copies = [
        send(
            chip_sum.at[pl.ds(pl.multiple_of(partner(x, i, nx) * rows_x, rows_x), rows_x)],
            from_x.at[i],
            sum_send.at[i],
            sum_recv.at[i],
            along_x(i),
        )
        for i in range(1, nx)
    ]
    total = chip_sum[pl.ds(pl.multiple_of(x * rows_x, rows_x), rows_x)]
    for i, copy in enumerate(copies):
        copy.wait_recv()
        total = total + from_x[i + 1]
    x_sum[...] = total

    rows_y = rows_x // ny
    copies = [
        send(
            x_sum.at[pl.ds(pl.multiple_of(partner(y, i, ny) * rows_y, rows_y), rows_y)],
            from_y.at[i],
            sum_send.at[3 + i],
            sum_recv.at[3 + i],
            along_y(i),
        )
        for i in range(1, ny)
    ]
    total = x_sum[pl.ds(pl.multiple_of(y * rows_y, rows_y), rows_y)]
    for i, copy in enumerate(copies):
        copy.wait_recv()
        total = total + from_y[i + 1]
    y_sum[...] = total

    far_first = sorted(range(1, nz), key=lambda d: -min(d, nz - d))
    copies = [
        send(y_sum, from_z.at[z], z_send.at[d - 1], z_recv.at[d - 1], along_z(d)) for d in far_first
    ]
    from_z[z] = total
    for copy in copies:
        copy.wait_recv()
    total = from_z[0]
    for i in range(1, nz):
        total = total + from_z[i]

    z_sum[...] = total
    here = pl.ds(pl.multiple_of(y * rows_y, rows_y), rows_y)
    copies = [
        send(z_sum, y_all.at[here], sum_send.at[6 + i], sum_recv.at[6 + i], along_y(i))
        for i in range(1, ny)
    ]
    y_all[here] = total
    for copy in copies:
        copy.wait_recv()
    here = pl.ds(pl.multiple_of(x * rows_x, rows_x), rows_x)
    copies = [
        send(y_all, x_all.at[here], sum_send.at[9 + i], sum_recv.at[9 + i], along_x(i))
        for i in range(1, nx)
    ]
    x_all[here] = y_all[...]
    for copy in copies:
        copy.wait_recv()
    copy = send(x_all, whole.at[c], sum_send.at[13], sum_recv.at[13], other_core)
    whole[c] = x_all[...]
    copy.wait_recv()
    total = jnp.concatenate([whole[0], whole[1, :, :BLOCK]], axis=1)
    query_grad_ref[...] = dot32(total, wk_ref[...])
    key_grad_ref[...] = dot32(total, wq_ref[...], TN)
    for copy in started:
        copy.wait_send()


def body(sizes, queries, key_states, samples, query_gate_weight, key_gate_weight):
    nz, nx, nyh = sizes
    ny = 2 * nyh
    rows_x = BLOCK // nx
    rows_y = rows_x // ny
    f32, bf16 = jnp.float32, jnp.bfloat16
    dma = pltpu.SemaphoreType.DMA
    vmem = pl.BlockSpec(memory_space=pltpu.VMEM)
    half = nz // 2
    return pl.pallas_call(
        functools.partial(kernel, sizes),
        out_shape=(
            jax.ShapeDtypeStruct((8, 8), f32),
            jax.ShapeDtypeStruct((BLOCK, BLOCK), f32),
            jax.ShapeDtypeStruct((3 * BLOCK, BLOCK), f32),
        ),
        in_specs=[vmem] * 5,
        out_specs=(vmem,) * 3,
        scratch_shapes=[
            pltpu.VMEM((nz, 2 * BLOCK, BLOCK), bf16),
            pltpu.VMEM((nz, 4, 8, BLOCK), f32),
            pltpu.VMEM((4, 64, BLOCK), bf16),
            pltpu.VMEM((2 * nz, 256), f32),
            pltpu.VMEM((2 * nz, 256), f32),
            pltpu.VMEM((4, 2 * nz, BLOCK), f32),
            pltpu.VMEM((4, 2 * nz, BLOCK), f32),
            pltpu.VMEM((2, BLOCK, 256), f32),
            pltpu.VMEM((BLOCK, 256), f32),
            pltpu.VMEM((BLOCK, 256), f32),
            pltpu.VMEM((4, rows_x, 256), f32),
            pltpu.VMEM((rows_x, 256), f32),
            pltpu.VMEM((4, rows_y, 256), f32),
            pltpu.VMEM((rows_y, 256), f32),
            pltpu.VMEM((nz, rows_y, 256), f32),
            pltpu.VMEM((rows_y, 256), f32),
            pltpu.VMEM((rows_x, 256), f32),
            pltpu.VMEM((BLOCK, 256), f32),
            pltpu.VMEM((2, BLOCK, 256), f32),
            dma((2, half, PIECES)),
            dma((2, half, PIECES)),
            dma((2, half)),
            dma((2, half)),
            dma((3, 3)),
            dma((3, 3)),
            dma((14,)),
            dma((14,)),
            dma((nz,)),
            dma((nz,)),
        ],
        compiler_params=pltpu.CompilerParams(collective_id=0, has_side_effects=True),
    )(queries, key_states, samples, query_gate_weight, key_gate_weight)


SEQ = ("yl", "z", "c")
KV = ("x", "yh")


def build(mesh, sizes):
    nz, nx, nyh = sizes
    torus = Mesh(mesh.devices.reshape(2, nz, 2, nx, nyh), (*SEQ, *KV))
    placed = (P(KV, SEQ, None), P(KV, SEQ, None), P(KV, SEQ), P(), P())
    return jax.shard_map(
        functools.partial(body, sizes),
        mesh=torus,
        in_specs=placed,
        out_specs=(P(KV, SEQ), P(), P()),
        check_vma=False,
    )


def solution(mesh):
    return build(mesh, (mesh.shape["seq"] // 4, mesh.shape["kv"] // 2, 2))
```

```python
import functools
import math

import jax
import jax.numpy as jnp
from jax import lax
from jax.experimental import pallas as pl
from jax.experimental.pallas import tpu as pltpu
from jax.sharding import Mesh
from jax.sharding import PartitionSpec as P

BLOCK = 128
MESH = pl.DeviceIdType.MESH
LOW = -1e30
highest = lax.Precision.HIGHEST
NN = (((1,), (0,)), ((), ()))
NT = (((1,), (1,)), ((), ()))
TN = (((0,), (0,)), ((), ()))


def dot32(a, b, dims=NN):
    return lax.dot_general(a, b, dims, precision=highest, preferred_element_type=jnp.float32)


def partner(place, apart, size):
    if apart == 0:
        return place
    if size == 2:
        return 1 - place
    return (place + 1 - 2 * (place % 2), (place + 2) % 4, 3 - place)[apart - 1]


def kernel(
    sizes,
    q_hbm,
    k_hbm,
    samples_hbm,
    wq_hbm,
    wk_hbm,
    loss_ref,
    total_ref,
    q_ref,
    keys,
    samples_ref,
    wq_ref,
    wk_ref,
    pooled,
    queries,
    packed,
    returned,
    part,
    from_core,
    chip_sum,
    from_xy,
    xy_sum,
    from_z,
    z_sum,
    xy_all,
    load_sem,
    query_send,
    query_recv,
    pool_send,
    pool_recv,
    back_send,
    back_recv,
    slice_send,
    slice_recv,
    core_send,
    core_recv,
    sum_send,
    sum_recv,
    all_send,
    all_recv,
    z_send,
    z_recv,
):
    nz, nx, nyh = sizes
    ny = 2 * nyh
    direct = nz // 4
    z, yl, c = lax.axis_index("z"), lax.axis_index("yl"), lax.axis_index("c")
    x, yh = lax.axis_index("x"), lax.axis_index("yh")
    y = 2 * yh + yl
    started = []

    def send(src, dst, send_sem, recv_sem, target):
        copy = pltpu.make_async_remote_copy(
            src_ref=src,
            dst_ref=dst,
            send_sem=send_sem,
            recv_sem=recv_sem,
            device_id=target,
            device_id_type=MESH,
        )
        copy.start()
        started.append(copy)
        return copy

    def along_z(step):
        return {"z": (z + step + nz) % nz}

    def in_slice(i):
        return {"yl": partner(yl, i // 2, 2), "c": partner(c, i % 2, 2)}

    def along_xy(n):
        other = partner(y, n % ny, ny)
        return {"x": partner(x, n // ny, nx), "yh": other // 2, "yl": other % 2}

    hops = (0, 1, 2, 1)
    others_xy = sorted(range(1, nx * ny), key=lambda n: -hops[n // ny] - hops[n % ny])
    other_core = {"c": 1 - c}

    near = [along_z(sign * d) for d in range(direct, 0, -1) for sign in (1, -1)]
    near += [along_xy(n) for n in others_xy]
    near += [in_slice(3), other_core]
    barrier = pltpu.get_barrier_semaphore()
    for target in near:
        pl.semaphore_signal(barrier, inc=1, device_id=target, device_id_type=MESH)

    loads = [
        pltpu.make_async_copy(src, dst, load_sem.at[n])
        for n, (src, dst) in enumerate(
            (
                (samples_hbm, samples_ref),
                (q_hbm, q_ref),
                (k_hbm.at[0], keys.at[0]),
                (wq_hbm, wq_ref),
                (wk_hbm, wk_ref),
            )
        )
    ]
    for load in loads:
        load.start()

    loads[0].wait()
    shard = (yl * nz + z) * 2 + c
    local = (samples_ref[...] - shard * (2 * BLOCK)).astype(jnp.float32)
    spread = jnp.concatenate([jnp.broadcast_to(local[h : h + 1], (8, 8)) for h in range(8)], axis=0)
    lanes8 = lax.broadcasted_iota(jnp.int32, (64, 8), 1)
    rows8 = lax.broadcasted_iota(jnp.int32, (64, 8), 0) % 8
    column = jnp.sum(jnp.where(lanes8 == rows8, spread, 0.0), axis=1, keepdims=True)
    tokens = lax.broadcasted_iota(jnp.int32, (8, 2 * BLOCK), 1)
    query_rows, pooled_rows = [], []
    loads[1].wait()
    for h in range(8):
        place = column[8 * h : 8 * h + 8].astype(jnp.int32)
        chosen = jnp.where(tokens == place, 1.0, 0.0)
        block = jnp.where(tokens // BLOCK == place // BLOCK, 1.0, 0.0)
        both = lax.dot_general(
            jnp.concatenate([chosen, block], axis=0).astype(jnp.bfloat16),
            q_ref[h],
            NN,
            preferred_element_type=jnp.float32,
        )
        query_rows.append(both[:8])
        pooled_rows.append(both[8:] * (1.0 / BLOCK))
    queries[0] = jnp.concatenate(query_rows, axis=0).astype(jnp.bfloat16)

    loads[2].wait()
    own = keys[0].astype(jnp.float32)
    blocks = (own[:BLOCK], own[BLOCK:])
    pooled[0, 0] = jnp.concatenate(
        [jnp.max(b, axis=0, keepdims=True) for b in blocks]
        + [jnp.min(b, axis=0, keepdims=True) for b in blocks]
        + [jnp.sum(b, axis=0, keepdims=True) * (1.0 / BLOCK) for b in blocks]
        + [jnp.zeros((2, own.shape[1]), jnp.float32)],
        axis=0,
    )

    pl.semaphore_wait(barrier, len(near))

    arrivals = {}

    def pass_on(held, step):
        at = (held + step + nz) % nz
        target = along_z(step)
        arrivals["query", at] = send(
            queries.at[held], queries.at[at], query_send.at[at], query_recv.at[at], target
        )
        arrivals["pool", at] = send(
            pooled.at[0, held], pooled.at[0, at], pool_send.at[at], pool_recv.at[at], target
        )

    for d in range(direct, 0, -1):
        for sign in (1, -1):
            pass_on(0, sign * d)
    keys_here = [
        send(
            keys.at[0],
            keys.at[i],
            slice_send.at[0, i - 1],
            slice_recv.at[0, i - 1],
            in_slice(i),
        )
        for i in (2, 3, 1)
    ]
    pooled_rows = jnp.concatenate(pooled_rows + [jnp.zeros((64, BLOCK), jnp.float32)], axis=0)
    loads[3].wait()
    gate_rows = dot32(pooled_rows, wq_ref[...])
    lanes = lax.broadcasted_iota(jnp.int32, (1, 256), 1)
    eye = lax.broadcasted_iota(jnp.int32, (64, 256), 0) == lax.broadcasted_iota(
        jnp.int32, (64, 256), 1
    )
    places = jnp.sum(jnp.where(eye, column, 0.0), axis=0, keepdims=True).astype(jnp.int32)
    places = jnp.where(lanes < 64, places, 2 * BLOCK - 1)

    for sign, last in ((1, direct), (-1, direct - 1)):
        held = (sign * direct + nz) % nz
        arrivals["query", held].wait_recv()
        arrivals["pool", held].wait_recv()
        for step in range(last, 0, -1):
            pass_on(held, sign * step)
    waited = {0, direct, nz - direct}

    for copy in keys_here:
        copy.wait_recv()
    exponent = math.log2(math.e) / math.sqrt(BLOCK)
    first = lax.broadcasted_iota(jnp.int32, (8, BLOCK), 1) < 64
    returns = {}

    def score(slots):
        for at in slots:
            if at not in waited:
                arrivals["query", at].wait_recv()
        rows = queries[slots[0] : slots[0] + 4].reshape(256, BLOCK)
        tops, sums = [], []
        for i in range(4):
            scores = lax.dot_general(keys[i], rows, NT, preferred_element_type=jnp.float32)
            if i == 0 and slots[0] == 0:
                token = lax.broadcasted_iota(jnp.int32, scores.shape, 0)
                scores = jnp.where(token <= places, scores, LOW)
            for b in range(2):
                block_scores = scores[b * BLOCK : (b + 1) * BLOCK]
                highest_score = jnp.max(block_scores, axis=0, keepdims=True)
                weights = jnp.exp2((block_scores - highest_score) * exponent)
                tops.append(highest_score)
                sums.append(jnp.sum(weights, axis=0, keepdims=True))
        tops = jnp.concatenate(tops, axis=0)
        sums = jnp.concatenate(sums, axis=0)
        for pair in range(2):
            top = tops[:, pair * BLOCK : (pair + 1) * BLOCK]
            mass = sums[:, pair * BLOCK : (pair + 1) * BLOCK]
            at = slots[0] + 2 * pair
            packed[at] = jnp.where(first, top, pltpu.roll(mass, 64, 1))
            packed[at + 1] = jnp.where(first, pltpu.roll(top, 64, 1), mass)
        for at in slots:
            if at:
                back = nz - at
                returns[back] = send(
                    packed.at[at],
                    returned.at[back],
                    back_send.at[back],
                    back_recv.at[back],
                    along_z(-at),
                )

    groups = [tuple(range(4 * g, 4 * g + 4)) for g in range(nz // 4)]
    if nz == 16:
        groups = [groups[0], groups[3], groups[1], groups[2]]
    for group in groups:
        score(group)
    returned[0] = packed[0]

    for at in range(1, nz):
        if at not in waited:
            arrivals["pool", at].wait_recv()
    pooled_here = [
        send(
            pooled.at[0],
            pooled.at[i],
            slice_send.at[1, i - 1],
            slice_recv.at[1, i - 1],
            in_slice(i),
        )
        for i in (2, 3, 1)
    ]
    loads[4].wait()
    for copy in pooled_here:
        copy.wait_recv()

    nb = 8 * nz
    pooled_keys = jnp.concatenate(
        [
            jnp.concatenate([pooled[i, :, 2 * kind + b, :] for kind in range(3)], axis=1)
            for i in range(4)
            for b in range(2)
        ],
        axis=0,
    )
    gate_key = dot32(pooled_keys, wk_ref[...])
    gate_scale = 1.0 / math.sqrt(BLOCK)
    logits = dot32(gate_key, gate_rows, NT) * gate_scale
    order = lax.broadcasted_iota(jnp.int32, (nb, BLOCK), 0)
    lane = lax.broadcasted_iota(jnp.int32, (nb, BLOCK), 1)
    i_of = order // (2 * nz)
    b_of = order // nz % 2
    z_of = (z - order % nz + nz) % nz
    yl_of = (yl + i_of // 2) % 2
    c_of = (c + i_of % 2) % 2
    block_of = ((yl_of * nz + z_of) * 2 + c_of) * 2 + b_of
    own_block = 2 * shard + places[:, :BLOCK] // BLOCK
    allowed = block_of <= own_block
    logit_top = jnp.max(jnp.where(allowed, logits, LOW), axis=0, keepdims=True)
    gate_weights = jnp.where(allowed, jnp.exp(logits - logit_top), 0.0)
    gate_total = jnp.sum(gate_weights, axis=0, keepdims=True)
    log_total = logit_top + jnp.log(gate_total)
    gate = gate_weights / gate_total

    for back in sorted(returns):
        returns[back].wait_recv()
    pairs = jnp.concatenate([returned[:, r, :] for r in range(8)], axis=0)
    sums = pltpu.roll(pairs, 64, 1)
    row_top = jnp.max(jnp.where(allowed, pairs, LOW), axis=0, keepdims=True)
    masses = jnp.where(allowed, sums * jnp.exp2((pairs - row_top) * exponent), 0.0)
    teacher = masses / jnp.sum(masses, axis=0, keepdims=True)
    losses = log_total - jnp.sum(jnp.where(allowed, teacher * logits, 0.0), axis=0, keepdims=True)
    delta = jnp.where(allowed & (lane < 64), (gate - teacher) * gate_scale, 0.0)

    block_query = dot32(delta, pooled_rows)
    local_sum = dot32(block_query, pooled_keys, TN)
    part[0] = local_sum[:, :256]
    part[1, :, :BLOCK] = local_sum[:, 256:]
    part[1, :, BLOCK:] = jnp.zeros((BLOCK, BLOCK), jnp.float32)
    copy = send(part.at[1 - c], from_core, core_send.at[0], core_recv.at[0], other_core)
    head_of = lax.broadcasted_iota(jnp.int32, (8, BLOCK), 1) // 8
    head = lax.broadcasted_iota(jnp.int32, (8, BLOCK), 0)
    row_of = lax.broadcasted_iota(jnp.int32, (BLOCK, BLOCK), 0) % 8
    row = lax.broadcasted_iota(jnp.int32, (BLOCK, BLOCK), 1)
    by_head = jnp.where(head_of == head, jnp.broadcast_to(losses, (8, BLOCK)), 0.0)
    loss_ref[...] = dot32(by_head, jnp.where(row_of == row, 1.0, 0.0))[:, :8]
    copy.wait_recv()
    chip_sum[...] = part[c] + from_core[...]

    rows_xy = BLOCK // (nx * ny)

    def rows_of(n):
        at = partner(x, n // ny, nx) * ny + partner(y, n % ny, ny)
        return pl.ds(pl.multiple_of(at * rows_xy, rows_xy), rows_xy)

    copies = [
        send(chip_sum.at[rows_of(n)], from_xy.at[n], sum_send.at[n], sum_recv.at[n], along_xy(n))
        for n in others_xy
    ]
    total = chip_sum[rows_of(0)]
    for copy, n in reversed(list(zip(copies, others_xy))):
        copy.wait_recv()
        total = total + from_xy[n]
    xy_sum[...] = total

    far_first = sorted(range(1, nz), key=lambda d: -min(d, nz - d))
    copies = [
        send(xy_sum, from_z.at[z], z_send.at[d], z_recv.at[d], along_z(d)) for d in far_first
    ]
    from_z[z] = total
    for copy in copies:
        copy.wait_recv()
    total = from_z[0]
    for i in range(1, nz):
        total = total + from_z[i]

    z_sum[...] = total
    copies = [
        send(z_sum, xy_all.at[rows_of(0)], all_send.at[n], all_recv.at[n], along_xy(n))
        for n in others_xy
    ]
    xy_all[rows_of(0)] = total
    for copy in copies:
        copy.wait_recv()
    copy = send(xy_all, total_ref.at[c], core_send.at[1], core_recv.at[1], other_core)
    total_ref[c] = xy_all[...]
    copy.wait_recv()
    for copy in started:
        copy.wait_send()


def finish(loss_ref, total_ref, wq_ref, wk_ref, row_loss_ref, query_grad_ref, key_grad_ref):
    total = jnp.concatenate([total_ref[0], total_ref[1, :, :BLOCK]], axis=1)
    query_grad_ref[...] = dot32(total, wk_ref[...])
    key_grad_ref[...] = dot32(total, wq_ref[...], TN)
    row_loss_ref[...] = loss_ref[...]


def body(sizes, queries, key_states, samples, query_gate_weight, key_gate_weight):
    nz, nx, nyh = sizes
    nxy = 2 * nx * nyh
    rows_xy = BLOCK // nxy
    f32, bf16 = jnp.float32, jnp.bfloat16
    dma = pltpu.SemaphoreType.DMA
    vmem = pl.BlockSpec(memory_space=pltpu.VMEM)
    losses, total = pl.pallas_call(
        functools.partial(kernel, sizes),
        out_shape=(
            jax.ShapeDtypeStruct((8, 8), f32),
            jax.ShapeDtypeStruct((2, BLOCK, 256), f32),
        ),
        in_specs=[pl.BlockSpec(memory_space=pl.ANY)] * 5,
        out_specs=(vmem,) * 2,
        scratch_shapes=[
            pltpu.VMEM((8, 2 * BLOCK, BLOCK), bf16),
            pltpu.VMEM((4, 2 * BLOCK, BLOCK), bf16),
            pltpu.VMEM((8, 8), jnp.int32),
            pltpu.VMEM((BLOCK, BLOCK), f32),
            pltpu.VMEM((3 * BLOCK, BLOCK), f32),
            pltpu.VMEM((4, nz, 8, BLOCK), f32),
            pltpu.VMEM((nz, 64, BLOCK), bf16),
            pltpu.VMEM((nz, 8, BLOCK), f32),
            pltpu.VMEM((nz, 8, BLOCK), f32),
            pltpu.VMEM((2, BLOCK, 256), f32),
            pltpu.VMEM((BLOCK, 256), f32),
            pltpu.VMEM((BLOCK, 256), f32),
            pltpu.VMEM((nxy, rows_xy, 256), f32),
            pltpu.VMEM((rows_xy, 256), f32),
            pltpu.VMEM((nz, rows_xy, 256), f32),
            pltpu.VMEM((rows_xy, 256), f32),
            pltpu.VMEM((BLOCK, 256), f32),
            dma((5,)),
            dma((nz,)),
            dma((nz,)),
            dma((nz,)),
            dma((nz,)),
            dma((nz,)),
            dma((nz,)),
            dma((2, 3)),
            dma((2, 3)),
            dma((2,)),
            dma((2,)),
            dma((nxy,)),
            dma((nxy,)),
            dma((nxy,)),
            dma((nxy,)),
            dma((nz,)),
            dma((nz,)),
        ],
        compiler_params=pltpu.CompilerParams(collective_id=0, has_side_effects=True),
    )(queries, key_states, samples, query_gate_weight, key_gate_weight)
    return pl.pallas_call(
        finish,
        out_shape=(
            jax.ShapeDtypeStruct((8, 8), f32),
            jax.ShapeDtypeStruct((BLOCK, BLOCK), f32),
            jax.ShapeDtypeStruct((3 * BLOCK, BLOCK), f32),
        ),
        in_specs=[vmem] * 4,
        out_specs=(vmem,) * 3,
    )(losses, total, query_gate_weight, key_gate_weight)


SEQ = ("yl", "z", "c")
KV = ("x", "yh")


def build(mesh, sizes):
    nz, nx, nyh = sizes
    torus = Mesh(mesh.devices.reshape(2, nz, 2, nx, nyh), (*SEQ, *KV))
    placed = (P(KV, SEQ, None), P(KV, SEQ, None), P(KV, SEQ), P(), P())
    return jax.shard_map(
        functools.partial(body, sizes),
        mesh=torus,
        in_specs=placed,
        out_specs=(P(KV, SEQ), P(), P()),
        check_vma=False,
    )


def solution(mesh):
    return build(mesh, (mesh.shape["seq"] // 4, mesh.shape["kv"] // 2, 2))
```

```python
import functools
import math

import jax
import jax.numpy as jnp
from jax import lax
from jax.experimental import pallas as pl
from jax.experimental.pallas import tpu as pltpu
from jax.sharding import Mesh
from jax.sharding import PartitionSpec as P

BLOCK = 128
MESH = pl.DeviceIdType.MESH
LOW = -1e30
highest = lax.Precision.HIGHEST
NN = (((1,), (0,)), ((), ()))
NT = (((1,), (1,)), ((), ()))
TN = (((0,), (0,)), ((), ()))
ROUTES = {
    4: ((1,), (1,), (), ((0, 1, 2, 3),)),
    8: ((1, 3), (1, -1), (1,), ((0, 1, 7, 3), (5, 4, 2, 6))),
    16: (
        (1, 2, 5),
        (3, 2, 1, -1, -2),
        (-2, -1, 1, 2),
        ((0, 1, 2, 15), (14, 5, 11, 4), (3, 12, 13, 6), (7, 8, 9, 10)),
    ),
}


def dot32(a, b, dims=NN):
    return lax.dot_general(a, b, dims, precision=highest, preferred_element_type=jnp.float32)


def partner(place, apart, size):
    if apart == 0:
        return place
    if size == 2:
        return 1 - place
    return (place + 1 - 2 * (place % 2), (place + 2) % 4, 3 - place)[apart - 1]


def kernel(
    sizes,
    q_hbm,
    k_hbm,
    samples_hbm,
    wq_hbm,
    wk_hbm,
    loss_ref,
    total_ref,
    wq_ref,
    wk_ref,
    q_ref,
    keys,
    samples_ref,
    pooled,
    queries,
    packed,
    returned,
    part,
    from_slice,
    slice_sum,
    from_z,
    z_sum,
    load_sem,
    query_send,
    query_recv,
    pool_send,
    pool_recv,
    keys_send,
    keys_recv,
    tile_send,
    tile_recv,
    back_send,
    back_recv,
    sum_send,
    sum_recv,
    z_send,
    z_recv,
    all_send,
    all_recv,
):
    nz, nx, nyh = sizes
    ny = 2 * nyh
    near_z, upper, lower, groups = ROUTES[nz]
    far = near_z[-1]
    z, yl, c = lax.axis_index("z"), lax.axis_index("yl"), lax.axis_index("c")
    x, yh = lax.axis_index("x"), lax.axis_index("yh")
    y = 2 * yh + yl
    def send(src, dst, send_sem, recv_sem, target):
        copy = pltpu.make_async_remote_copy(
            src_ref=src,
            dst_ref=dst,
            send_sem=send_sem,
            recv_sem=recv_sem,
            device_id=target,
            device_id_type=MESH,
        )
        copy.start()
        return copy

    def wait_for(ref, sem):
        pltpu.make_async_copy(ref, ref, sem).wait()

    def along_z(step):
        return {"z": (z + step + nz) % nz}

    def in_slice(i):
        return {"yl": partner(yl, i // 2, 2), "c": partner(c, i % 2, 2)}

    def along_xy(n):
        other = partner(y, n // 2 % ny, ny)
        return {
            "x": partner(x, n // (2 * ny), nx),
            "yh": other // 2,
            "yl": other % 2,
            "c": partner(c, n % 2, 2),
        }

    slice_size = 2 * nx * ny
    hops = (0, 1, 2, 1)
    others = sorted(
        range(1, slice_size), key=lambda n: -hops[n // (2 * ny)] - hops[n // 2 % ny]
    )
    touched = sorted({*near_z, *map(abs, upper), *map(abs, lower)}, reverse=True)
    near = [along_z(sign * d) for d in touched for sign in (1, -1)]
    near += [along_xy(n) for n in others]
    loads = [
        pltpu.make_async_copy(src, dst, load_sem.at[n])
        for n, (src, dst) in enumerate(
            (
                (samples_hbm, samples_ref),
                (q_hbm, q_ref),
                (k_hbm.at[0], keys.at[0]),
                (wq_hbm, wq_ref),
                (wk_hbm, wk_ref),
            )
        )
    ]
    for load in loads:
        load.start()

    barrier = pltpu.get_barrier_semaphore()
    for target in near:
        pl.semaphore_signal(barrier, inc=1, device_id=target, device_id_type=MESH)

    loads[2].wait()
    own = keys[0].astype(jnp.float32)
    blocks = (own[:BLOCK], own[BLOCK:])
    pooled[0, 0] = jnp.concatenate(
        [jnp.max(b, axis=0, keepdims=True) for b in blocks]
        + [jnp.min(b, axis=0, keepdims=True) for b in blocks]
        + [jnp.sum(b, axis=0, keepdims=True) * (1.0 / BLOCK) for b in blocks]
        + [jnp.zeros((2, own.shape[1]), jnp.float32)],
        axis=0,
    )

    loads[0].wait()
    shard = (yl * nz + z) * 2 + c
    local = (samples_ref[...] - shard * (2 * BLOCK)).astype(jnp.float32)
    spread = jnp.concatenate([jnp.broadcast_to(local[h : h + 1], (8, 8)) for h in range(8)], axis=0)
    lanes8 = lax.broadcasted_iota(jnp.int32, (64, 8), 1)
    rows8 = lax.broadcasted_iota(jnp.int32, (64, 8), 0) % 8
    column = jnp.sum(jnp.where(lanes8 == rows8, spread, 0.0), axis=1, keepdims=True)
    tokens = lax.broadcasted_iota(jnp.int32, (8, 2 * BLOCK), 1)
    query_rows, pooled_rows = [], []
    loads[1].wait()
    for h in range(8):
        place = column[8 * h : 8 * h + 8].astype(jnp.int32)
        chosen = jnp.where(tokens == place, 1.0, 0.0)
        block = jnp.where(tokens // BLOCK == place // BLOCK, 1.0, 0.0)
        both = lax.dot_general(
            jnp.concatenate([chosen, block], axis=0).astype(jnp.bfloat16),
            q_ref[h],
            NN,
            preferred_element_type=jnp.float32,
        )
        query_rows.append(both[:8])
        pooled_rows.append(both[8:] * (1.0 / BLOCK))
    queries[0] = jnp.concatenate(query_rows, axis=0).astype(jnp.bfloat16)

    pl.semaphore_wait(barrier, len(near))

    far_places = (far, nz - far)
    group_of = {at: g for g, group in enumerate(groups) for at in group}
    group_of.update({at: len(groups) + n for n, at in enumerate(far_places)})
    waits = [[at for at in group if at not in (0, *far_places)] for group in groups]

    def pass_pool(held, step):
        at = (held + step + nz) % nz
        send(
            pooled.at[0, held],
            pooled.at[0, at],
            pool_send,
            pool_recv.at[group_of[at]],
            along_z(step),
        )

    def pass_query(held, step):
        at = (held + step + nz) % nz
        send(
            queries.at[held],
            queries.at[at],
            query_send,
            query_recv.at[group_of[at]],
            along_z(step),
        )

    for d in reversed(near_z):
        for sign in (1, -1):
            pass_query(0, sign * d)
    for d in reversed(near_z):
        for sign in (1, -1):
            pass_pool(0, sign * d)
    for i in (2, 3, 1):
        send(keys.at[0], keys.at[i], keys_send, keys_recv, in_slice(i))
    pooled_rows = jnp.concatenate(pooled_rows + [jnp.zeros((64, BLOCK), jnp.float32)], axis=0)
    loads[3].wait()
    gate_rows = dot32(pooled_rows, wq_ref[...])
    lanes = lax.broadcasted_iota(jnp.int32, (1, 256), 1)
    eye = lax.broadcasted_iota(jnp.int32, (64, 256), 0) == lax.broadcasted_iota(
        jnp.int32, (64, 256), 1
    )
    places = jnp.sum(jnp.where(eye, column, 0.0), axis=0, keepdims=True).astype(jnp.int32)
    places = jnp.where(lanes < 64, places, 2 * BLOCK - 1)

    for pass_on, kept, recv in (
        (pass_query, queries, query_recv),
        (pass_pool, pooled.at[0], pool_recv),
    ):
        for held, steps in zip(far_places, (upper, lower)):
            wait_for(kept.at[held], recv.at[group_of[held]])
            for step in steps:
                pass_on(held, step)

    wait_for(keys.at[1:4], keys_recv)
    exponent = math.log2(math.e) / math.sqrt(BLOCK)
    first = lax.broadcasted_iota(jnp.int32, (8, BLOCK), 1) < 64

    def score(slots, waited):
        wait_for(queries.at[: len(waited)], query_recv.at[group_of[waited[0]]])
        rows = jnp.concatenate([queries[at] for at in slots], axis=0)
        tops, sums = [], []
        for i in range(4):
            scores = lax.dot_general(keys[i], rows, NT, preferred_element_type=jnp.float32)
            if i == 0 and slots[0] == 0:
                token = lax.broadcasted_iota(jnp.int32, scores.shape, 0)
                scores = jnp.where(token <= places, scores, LOW)
            for b in range(2):
                block_scores = scores[b * BLOCK : (b + 1) * BLOCK]
                highest_score = jnp.max(block_scores, axis=0, keepdims=True)
                weights = jnp.exp2((block_scores - highest_score) * exponent)
                tops.append(highest_score)
                sums.append(jnp.sum(weights, axis=0, keepdims=True))
        tops = jnp.concatenate(tops, axis=0)
        sums = jnp.concatenate(sums, axis=0)
        for pair in range(2):
            top = tops[:, pair * BLOCK : (pair + 1) * BLOCK]
            mass = sums[:, pair * BLOCK : (pair + 1) * BLOCK]
            packed[slots[2 * pair]] = jnp.where(first, top, pltpu.roll(mass, 64, 1))
            packed[slots[2 * pair + 1]] = jnp.where(first, pltpu.roll(top, 64, 1), mass)
        for at in slots:
            if at:
                back = nz - at
                send(packed.at[at], returned.at[back], back_send, back_recv, along_z(-at))

    for group, waited in zip(groups, waits):
        score(group, waited)
        wait_for(pooled.at[0, : len(waited)], pool_recv.at[group_of[waited[0]]])
        for at in group:
            for i in (2, 3, 1):
                send(pooled.at[0, at], pooled.at[i, at], tile_send, tile_recv, in_slice(i))
    returned[0] = packed[0]
    loads[4].wait()
    wait_for(pooled.at[1:4], tile_recv)

    nb = 8 * nz
    pooled_keys = jnp.concatenate(
        [
            jnp.concatenate([pooled[i, :, 2 * kind + b, :] for kind in range(3)], axis=1)
            for i in range(4)
            for b in range(2)
        ],
        axis=0,
    )
    gate_key = dot32(pooled_keys, wk_ref[...])
    gate_scale = 1.0 / math.sqrt(BLOCK)
    logits = dot32(gate_key, gate_rows, NT) * gate_scale
    order = lax.broadcasted_iota(jnp.int32, (nb, BLOCK), 0)
    lane = lax.broadcasted_iota(jnp.int32, (nb, BLOCK), 1)
    i_of = order // (2 * nz)
    b_of = order // nz % 2
    z_of = (z - order % nz + nz) % nz
    yl_of = (yl + i_of // 2) % 2
    c_of = (c + i_of % 2) % 2
    block_of = ((yl_of * nz + z_of) * 2 + c_of) * 2 + b_of
    own_block = 2 * shard + places[:, :BLOCK] // BLOCK
    allowed = block_of <= own_block
    logit_top = jnp.max(jnp.where(allowed, logits, LOW), axis=0, keepdims=True)
    gate_weights = jnp.where(allowed, jnp.exp(logits - logit_top), 0.0)
    gate_total = jnp.sum(gate_weights, axis=0, keepdims=True)
    log_total = logit_top + jnp.log(gate_total)
    gate = gate_weights / gate_total

    wait_for(returned.at[1:], back_recv)
    pairs = jnp.concatenate([returned[:, r, :] for r in range(8)], axis=0)
    sums = pltpu.roll(pairs, 64, 1)
    row_top = jnp.max(jnp.where(allowed, pairs, LOW), axis=0, keepdims=True)
    masses = jnp.where(allowed, sums * jnp.exp2((pairs - row_top) * exponent), 0.0)
    teacher = masses / jnp.sum(masses, axis=0, keepdims=True)
    losses = log_total - jnp.sum(jnp.where(allowed, teacher * logits, 0.0), axis=0, keepdims=True)
    delta = jnp.where(allowed & (lane < 64), (gate - teacher) * gate_scale, 0.0)

    block_query = dot32(delta, pooled_rows)
    local_sum = dot32(block_query, pooled_keys, TN)
    rows = BLOCK // slice_size
    for n in range(slice_size):
        for kind in range(3):
            part[n, kind] = local_sum[rows * n : rows * (n + 1), BLOCK * kind : BLOCK * (kind + 1)]

    def place_of(n):
        at = partner(x, n // (2 * ny), nx) * ny + partner(y, n // 2 % ny, ny)
        return 2 * at + partner(c, n % 2, 2)

    for n in others:
        send(part.at[place_of(n)], from_slice.at[n], sum_send, sum_recv, along_xy(n))
    head_of = lax.broadcasted_iota(jnp.int32, (8, BLOCK), 1) // 8
    head = lax.broadcasted_iota(jnp.int32, (8, BLOCK), 0)
    row_of = lax.broadcasted_iota(jnp.int32, (BLOCK, BLOCK), 0) % 8
    row = lax.broadcasted_iota(jnp.int32, (BLOCK, BLOCK), 1)
    by_head = jnp.where(head_of == head, jnp.broadcast_to(losses, (8, BLOCK)), 0.0)
    loss_ref[...] = dot32(by_head, jnp.where(row_of == row, 1.0, 0.0))[:, :8]
    total = part[place_of(0)]
    wait_for(from_slice.at[1:], sum_recv)
    for n in range(1, slice_size):
        total = total + from_slice[n]
    slice_sum[...] = total

    far_first = sorted(range(1, nz), key=lambda d: -min(d, nz - d))
    for d in far_first:
        send(slice_sum, from_z.at[z], z_send, z_recv, along_z(d))
    from_z[z] = total
    wait_for(from_z.at[1:], z_recv)
    total = from_z[0]
    for i in range(1, nz):
        total = total + from_z[i]

    z_sum[...] = total
    for n in others:
        send(z_sum, total_ref.at[place_of(0)], all_send, all_recv, along_xy(n))
    total_ref[place_of(0)] = total
    wait_for(queries.at[1:], query_send)
    wait_for(pooled.at[0, 1:], pool_send)
    wait_for(keys.at[1:], keys_send)
    wait_for(packed.at[1:], back_send)
    wait_for(pooled.at[1:], tile_send)
    wait_for(part.at[1:], sum_send)
    wait_for(from_z.at[1:], z_send)
    wait_for(from_slice.at[1:], all_send)
    wait_for(from_slice.at[1:], all_recv)


def finish(loss_ref, total_ref, wq_ref, wk_ref, row_loss_ref, query_grad_ref, key_grad_ref):
    total = jnp.concatenate(
        [
            jnp.concatenate([total_ref[n, kind] for n in range(total_ref.shape[0])], axis=0)
            for kind in range(3)
        ],
        axis=1,
    )
    query_grad_ref[...] = dot32(total, wk_ref[...])
    key_grad_ref[...] = dot32(total, wq_ref[...], TN)
    row_loss_ref[...] = loss_ref[...]


def body(sizes, queries, key_states, samples, query_gate_weight, key_gate_weight):
    nz, nx, nyh = sizes
    slice_size = 4 * nx * nyh
    tile = (3, BLOCK // slice_size, BLOCK)
    f32, bf16 = jnp.float32, jnp.bfloat16
    dma = pltpu.SemaphoreType.DMA
    vmem = pl.BlockSpec(memory_space=pltpu.VMEM)
    handed = pl.pallas_call(
        functools.partial(kernel, sizes),
        out_shape=(
            pltpu.VMEM((8, 8), f32),
            pltpu.VMEM((slice_size, *tile), f32),
            pltpu.VMEM((BLOCK, BLOCK), f32),
            pltpu.VMEM((3 * BLOCK, BLOCK), f32),
        ),
        in_specs=[pl.BlockSpec(memory_space=pl.ANY)] * 5,
        out_specs=(vmem,) * 4,
        scratch_shapes=[
            pltpu.VMEM((8, 2 * BLOCK, BLOCK), bf16),
            pltpu.VMEM((4, 2 * BLOCK, BLOCK), bf16),
            pltpu.VMEM((8, 8), jnp.int32),
            pltpu.VMEM((4, nz, 8, BLOCK), f32),
            pltpu.VMEM((nz, 64, BLOCK), bf16),
            pltpu.VMEM((nz, 8, BLOCK), f32),
            pltpu.VMEM((nz, 8, BLOCK), f32),
            pltpu.VMEM((slice_size, *tile), f32),
            pltpu.VMEM((slice_size, *tile), f32),
            pltpu.VMEM(tile, f32),
            pltpu.VMEM((nz, *tile), f32),
            pltpu.VMEM(tile, f32),
            dma((5,)),
            dma,
            dma((len(ROUTES[nz][3]) + 2,)),
            dma,
            dma((len(ROUTES[nz][3]) + 2,)),
        ]
        + [dma] * 12,
        compiler_params=pltpu.CompilerParams(collective_id=0, has_side_effects=True),
    )(queries, key_states, samples, query_gate_weight, key_gate_weight)
    return pl.pallas_call(
        finish,
        out_shape=(
            jax.ShapeDtypeStruct((8, 8), f32),
            jax.ShapeDtypeStruct((BLOCK, BLOCK), f32),
            jax.ShapeDtypeStruct((3 * BLOCK, BLOCK), f32),
        ),
        in_specs=[vmem] * 4,
        out_specs=(vmem,) * 3,
    )(*[pltpu.with_memory_space_constraint(a, pltpu.VMEM) for a in handed])


SEQ = ("yl", "z", "c")
KV = ("x", "yh")


def build(mesh, sizes):
    nz, nx, nyh = sizes
    torus = Mesh(mesh.devices.reshape(2, nz, 2, nx, nyh), (*SEQ, *KV))
    placed = (P(KV, SEQ, None), P(KV, SEQ, None), P(KV, SEQ), P(), P())
    return jax.shard_map(
        functools.partial(body, sizes),
        mesh=torus,
        in_specs=placed,
        out_specs=(P(KV, SEQ), P(), P()),
        check_vma=False,
    )


def solution(mesh):
    return build(mesh, (mesh.shape["seq"] // 4, mesh.shape["kv"] // 2, 2))
```

```python
import functools
import math

import jax
import jax.numpy as jnp
from jax import lax
from jax.experimental import pallas as pl
from jax.experimental.pallas import tpu as pltpu
from jax.sharding import Mesh
from jax.sharding import PartitionSpec as P

BLOCK = 128
MESH = pl.DeviceIdType.MESH
LOW = -1e30
highest = lax.Precision.HIGHEST
NN = (((1,), (0,)), ((), ()))
NT = (((1,), (1,)), ((), ()))
TN = (((0,), (0,)), ((), ()))
ROUTES = {
    4: ((1,), (1,), (), ((0, 1, 2, 3),)),
    8: ((1, 3), (1, -1), (1,), ((0, 1, 7, 3), (5, 4, 2, 6))),
    16: (
        (1, 2, 5),
        (3, 2, 1, -1, -2),
        (-2, -1, 1, 2),
        ((0, 1, 2, 15), (14, 5, 11, 6), (7, 8, 9, 10), (4, 3, 12, 13)),
    ),
}


def dot32(a, b, dims=NN):
    return lax.dot_general(a, b, dims, precision=highest, preferred_element_type=jnp.float32)


def partner(place, apart, size):
    if apart == 0:
        return place
    if size == 2:
        return 1 - place
    return (place + 1 - 2 * (place % 2), (place + 2) % 4, 3 - place)[apart - 1]


def kernel(
    sizes,
    q_hbm,
    k_hbm,
    samples_hbm,
    wq_hbm,
    wk_hbm,
    loss_ref,
    total_ref,
    wq_ref,
    wk_ref,
    q_ref,
    keys,
    samples_ref,
    pooled,
    queries,
    packed,
    returned,
    part,
    from_slice,
    slice_sum,
    from_z,
    z_sum,
    load_sem,
    query_send,
    query_recv,
    pool_send,
    pool_recv,
    keys_send,
    keys_recv,
    tile_send,
    tile_recv,
    back_send,
    back_recv,
    sum_send,
    sum_recv,
    z_send,
    z_recv,
    all_send,
    all_recv,
):
    nz, nx, nyh = sizes
    ny = 2 * nyh
    near_z, upper, lower, groups = ROUTES[nz]
    far = near_z[-1]
    z, yl, c = lax.axis_index("z"), lax.axis_index("yl"), lax.axis_index("c")
    x, yh = lax.axis_index("x"), lax.axis_index("yh")
    y = 2 * yh + yl
    def send(src, dst, send_sem, recv_sem, target):
        copy = pltpu.make_async_remote_copy(
            src_ref=src,
            dst_ref=dst,
            send_sem=send_sem,
            recv_sem=recv_sem,
            device_id=target,
            device_id_type=MESH,
        )
        copy.start()
        return copy

    def wait_for(ref, sem):
        pltpu.make_async_copy(ref, ref, sem).wait()

    def along_z(step):
        return {"z": (z + step + nz) % nz}

    def in_slice(i):
        return {"yl": partner(yl, i // 2, 2), "c": partner(c, i % 2, 2)}

    def along_xy(n):
        other = partner(y, n // 2 % ny, ny)
        return {
            "x": partner(x, n // (2 * ny), nx),
            "yh": other // 2,
            "yl": other % 2,
            "c": partner(c, n % 2, 2),
        }

    slice_size = 2 * nx * ny
    hops = (0, 1, 2, 1)
    others = sorted(
        range(1, slice_size), key=lambda n: -hops[n // (2 * ny)] - hops[n // 2 % ny]
    )
    touched = sorted({*near_z, *map(abs, upper), *map(abs, lower)}, reverse=True)
    near = [along_z(sign * d) for d in touched for sign in (1, -1)]
    near += [along_xy(n) for n in others]
    loads = [
        pltpu.make_async_copy(src, dst, load_sem.at[n])
        for n, (src, dst) in enumerate(
            (
                (samples_hbm, samples_ref),
                (q_hbm, q_ref),
                (k_hbm.at[0], keys.at[0]),
                (wq_hbm, wq_ref),
                (wk_hbm, wk_ref),
            )
        )
    ]
    for load in loads:
        load.start()

    barrier = pltpu.get_barrier_semaphore()
    for target in near:
        pl.semaphore_signal(barrier, inc=1, device_id=target, device_id_type=MESH)

    loads[2].wait()
    own = keys[0].astype(jnp.float32)
    blocks = (own[:BLOCK], own[BLOCK:])
    pooled[0, 0] = jnp.concatenate(
        [jnp.max(b, axis=0, keepdims=True) for b in blocks]
        + [jnp.min(b, axis=0, keepdims=True) for b in blocks]
        + [jnp.sum(b, axis=0, keepdims=True) * (1.0 / BLOCK) for b in blocks]
        + [jnp.zeros((2, own.shape[1]), jnp.float32)],
        axis=0,
    )

    loads[0].wait()
    shard = (yl * nz + z) * 2 + c
    local = (samples_ref[...] - shard * (2 * BLOCK)).astype(jnp.float32)
    spread = jnp.concatenate([jnp.broadcast_to(local[h : h + 1], (8, 8)) for h in range(8)], axis=0)
    lanes8 = lax.broadcasted_iota(jnp.int32, (64, 8), 1)
    rows8 = lax.broadcasted_iota(jnp.int32, (64, 8), 0) % 8
    column = jnp.sum(jnp.where(lanes8 == rows8, spread, 0.0), axis=1, keepdims=True)
    tokens = lax.broadcasted_iota(jnp.int32, (8, 2 * BLOCK), 1)
    query_rows, pooled_rows = [], []
    loads[1].wait()
    for h in range(8):
        place = column[8 * h : 8 * h + 8].astype(jnp.int32)
        chosen = jnp.where(tokens == place, 1.0, 0.0)
        block = jnp.where(tokens // BLOCK == place // BLOCK, 1.0, 0.0)
        both = lax.dot_general(
            jnp.concatenate([chosen, block], axis=0).astype(jnp.bfloat16),
            q_ref[h],
            NN,
            preferred_element_type=jnp.float32,
        )
        query_rows.append(both[:8])
        pooled_rows.append(both[8:] * (1.0 / BLOCK))
    queries[0] = jnp.concatenate(query_rows, axis=0).astype(jnp.bfloat16)

    pl.semaphore_wait(barrier, len(near))

    far_places = (far, nz - far)
    group_of = {at: g for g, group in enumerate(groups) for at in group}
    group_of.update({at: len(groups) + n for n, at in enumerate(far_places)})
    waits = [[at for at in group if at not in (0, *far_places)] for group in groups]

    def pass_pool(held, step):
        at = (held + step + nz) % nz
        send(
            pooled.at[0, held, :6],
            pooled.at[0, at, :6],
            pool_send,
            pool_recv.at[group_of[at]],
            along_z(step),
        )

    def pass_query(held, step):
        at = (held + step + nz) % nz
        send(
            queries.at[held],
            queries.at[at],
            query_send,
            query_recv.at[group_of[at]],
            along_z(step),
        )

    for d in reversed(near_z):
        for sign in (1, -1):
            pass_query(0, sign * d)
    for d in reversed(near_z):
        for sign in (1, -1):
            pass_pool(0, sign * d)
    for i in (2, 3, 1):
        send(keys.at[0], keys.at[i], keys_send, keys_recv, in_slice(i))
    pooled_rows = jnp.concatenate(pooled_rows + [jnp.zeros((64, BLOCK), jnp.float32)], axis=0)
    loads[3].wait()
    gate_rows = dot32(pooled_rows, wq_ref[...])
    pooled_columns = pooled_rows.T
    lanes = lax.broadcasted_iota(jnp.int32, (1, 256), 1)
    eye = lax.broadcasted_iota(jnp.int32, (64, 256), 0) == lax.broadcasted_iota(
        jnp.int32, (64, 256), 1
    )
    places = jnp.sum(jnp.where(eye, column, 0.0), axis=0, keepdims=True).astype(jnp.int32)
    places = jnp.where(lanes < 64, places, 2 * BLOCK - 1)

    for pass_on, kept, recv in (
        (pass_query, queries, query_recv),
        (pass_pool, pooled.at[0], pool_recv),
    ):
        for held, steps in zip(far_places, (upper, lower)):
            wait_for(kept.at[held] if kept is queries else kept.at[held, :6], recv.at[group_of[held]])
            for step in steps:
                pass_on(held, step)

    wait_for(keys.at[1:4], keys_recv)
    exponent = math.log2(math.e) / math.sqrt(BLOCK)
    first = lax.broadcasted_iota(jnp.int32, (8, BLOCK), 1) < 64

    def score(slots, waited):
        wait_for(queries.at[: len(waited)], query_recv.at[group_of[waited[0]]])
        rows = jnp.concatenate([queries[at] for at in slots], axis=0)
        tops, sums = [], []
        for i in range(4):
            scores = lax.dot_general(keys[i], rows, NT, preferred_element_type=jnp.float32)
            if i == 0 and slots[0] == 0:
                token = lax.broadcasted_iota(jnp.int32, scores.shape, 0)
                scores = jnp.where(token <= places, scores, LOW)
            for b in range(2):
                block_scores = scores[b * BLOCK : (b + 1) * BLOCK]
                highest_score = jnp.max(block_scores, axis=0, keepdims=True)
                weights = jnp.exp2((block_scores - highest_score) * exponent)
                tops.append(highest_score)
                sums.append(jnp.sum(weights, axis=0, keepdims=True))
        tops = jnp.concatenate(tops, axis=0)
        sums = jnp.concatenate(sums, axis=0)
        for pair in range(2):
            top = tops[:, pair * BLOCK : (pair + 1) * BLOCK]
            mass = sums[:, pair * BLOCK : (pair + 1) * BLOCK]
            packed[slots[2 * pair]] = jnp.where(first, top, pltpu.roll(mass, 64, 1))
            packed[slots[2 * pair + 1]] = jnp.where(first, pltpu.roll(top, 64, 1), mass)
        for at in slots:
            if at:
                back = nz - at
                send(packed.at[at], returned.at[back], back_send, back_recv, along_z(-at))

    def share_tiles(group, waited):
        wait_for(pooled.at[0, : len(waited), :6], pool_recv.at[group_of[waited[0]]])
        for at in group:
            for i in (2, 3, 1):
                send(
                    pooled.at[0, at, :6], pooled.at[i, at, :6], tile_send, tile_recv, in_slice(i)
                )

    for n, (group, waited) in enumerate(zip(groups, waits)):
        score(group, waited)
        if n < len(groups) - 2:
            share_tiles(group, waited)
    for group, waited in list(zip(groups, waits))[-2:]:
        share_tiles(group, waited)
    returned[0] = packed[0]
    loads[4].wait()
    wait_for(pooled.at[1:4, :, :6], tile_recv)

    nb = 8 * nz
    pooled_keys = jnp.concatenate(
        [
            jnp.concatenate([pooled[i, :, 2 * kind + b, :] for kind in range(3)], axis=1)
            for i in range(4)
            for b in range(2)
        ],
        axis=0,
    )
    gate_key = dot32(pooled_keys, wk_ref[...])
    gate_scale = 1.0 / math.sqrt(BLOCK)
    logits = dot32(gate_key, gate_rows, NT) * gate_scale
    order = lax.broadcasted_iota(jnp.int32, (nb, BLOCK), 0)
    lane = lax.broadcasted_iota(jnp.int32, (nb, BLOCK), 1)
    i_of = order // (2 * nz)
    b_of = order // nz % 2
    z_of = (z - order % nz + nz) % nz
    yl_of = (yl + i_of // 2) % 2
    c_of = (c + i_of % 2) % 2
    block_of = ((yl_of * nz + z_of) * 2 + c_of) * 2 + b_of
    own_block = 2 * shard + places[:, :BLOCK] // BLOCK
    allowed = block_of <= own_block
    logit_top = jnp.max(jnp.where(allowed, logits, LOW), axis=0, keepdims=True)
    gate_weights = jnp.where(allowed, jnp.exp(logits - logit_top), 0.0)
    gate_total = jnp.sum(gate_weights, axis=0, keepdims=True)
    log_total = logit_top + jnp.log(gate_total)
    gate = gate_weights / gate_total

    wait_for(returned.at[1:], back_recv)
    pairs = jnp.concatenate([returned[:, r, :] for r in range(8)], axis=0)
    sums = pltpu.roll(pairs, 64, 1)
    row_top = jnp.max(jnp.where(allowed, pairs, LOW), axis=0, keepdims=True)
    masses = jnp.where(allowed, sums * jnp.exp2((pairs - row_top) * exponent), 0.0)
    teacher = masses / jnp.sum(masses, axis=0, keepdims=True)
    losses = log_total - jnp.sum(jnp.where(allowed, teacher * logits, 0.0), axis=0, keepdims=True)
    delta = jnp.where(allowed & (lane < 64), (gate - teacher) * gate_scale, 0.0)

    block_query = dot32(pooled_columns, delta, NT)
    local_sum = dot32(block_query, pooled_keys)
    rows = BLOCK // slice_size
    for n in range(slice_size):
        for kind in range(3):
            part[n, kind] = local_sum[rows * n : rows * (n + 1), BLOCK * kind : BLOCK * (kind + 1)]

    def place_of(n):
        at = partner(x, n // (2 * ny), nx) * ny + partner(y, n // 2 % ny, ny)
        return 2 * at + partner(c, n % 2, 2)

    for n in others:
        send(part.at[place_of(n)], from_slice.at[n], sum_send, sum_recv, along_xy(n))
    head_of = lax.broadcasted_iota(jnp.int32, (8, BLOCK), 1) // 8
    head = lax.broadcasted_iota(jnp.int32, (8, BLOCK), 0)
    row_of = lax.broadcasted_iota(jnp.int32, (BLOCK, BLOCK), 0) % 8
    row = lax.broadcasted_iota(jnp.int32, (BLOCK, BLOCK), 1)
    by_head = jnp.where(head_of == head, jnp.broadcast_to(losses, (8, BLOCK)), 0.0)
    loss_ref[...] = dot32(by_head, jnp.where(row_of == row, 1.0, 0.0))[:, :8]
    total = part[place_of(0)]
    wait_for(from_slice.at[1:], sum_recv)
    for n in range(1, slice_size):
        total = total + from_slice[n]
    slice_sum[...] = total

    far_first = sorted(range(1, nz), key=lambda d: -min(d, nz - d))
    for d in far_first:
        send(slice_sum, from_z.at[z], z_send, z_recv, along_z(d))
    from_z[z] = total
    wait_for(from_z.at[1:], z_recv)
    total = from_z[0]
    for i in range(1, nz):
        total = total + from_z[i]

    z_sum[...] = total
    for n in others:
        send(z_sum, total_ref.at[place_of(0)], all_send, all_recv, along_xy(n))
    total_ref[place_of(0)] = total
    wait_for(queries.at[1:], query_send)
    wait_for(pooled.at[0, 1:, :6], pool_send)
    wait_for(keys.at[1:], keys_send)
    wait_for(packed.at[1:], back_send)
    wait_for(pooled.at[1:, :, :6], tile_send)
    wait_for(part.at[1:], sum_send)
    wait_for(from_z.at[1:], z_send)
    wait_for(from_slice.at[1:], all_send)
    wait_for(from_slice.at[1:], all_recv)


def finish(loss_ref, total_ref, wq_ref, wk_ref, row_loss_ref, query_grad_ref, key_grad_ref):
    total = jnp.concatenate(
        [
            jnp.concatenate([total_ref[n, kind] for n in range(total_ref.shape[0])], axis=0)
            for kind in range(3)
        ],
        axis=1,
    )
    query_grad_ref[...] = dot32(total, wk_ref[...])
    key_grad_ref[...] = dot32(total, wq_ref[...], TN)
    row_loss_ref[...] = loss_ref[...]


def body(sizes, queries, key_states, samples, query_gate_weight, key_gate_weight):
    nz, nx, nyh = sizes
    slice_size = 4 * nx * nyh
    tile = (3, BLOCK // slice_size, BLOCK)
    f32, bf16 = jnp.float32, jnp.bfloat16
    dma = pltpu.SemaphoreType.DMA
    vmem = pl.BlockSpec(memory_space=pltpu.VMEM)
    handed = pl.pallas_call(
        functools.partial(kernel, sizes),
        out_shape=(
            pltpu.VMEM((8, 8), f32),
            pltpu.VMEM((slice_size, *tile), f32),
            pltpu.VMEM((BLOCK, BLOCK), f32),
            pltpu.VMEM((3 * BLOCK, BLOCK), f32),
        ),
        in_specs=[pl.BlockSpec(memory_space=pl.ANY)] * 5,
        out_specs=(vmem,) * 4,
        scratch_shapes=[
            pltpu.VMEM((8, 2 * BLOCK, BLOCK), bf16),
            pltpu.VMEM((4, 2 * BLOCK, BLOCK), bf16),
            pltpu.VMEM((8, 8), jnp.int32),
            pltpu.VMEM((4, nz, 8, BLOCK), f32),
            pltpu.VMEM((nz, 64, BLOCK), bf16),
            pltpu.VMEM((nz, 8, BLOCK), f32),
            pltpu.VMEM((nz, 8, BLOCK), f32),
            pltpu.VMEM((slice_size, *tile), f32),
            pltpu.VMEM((slice_size, *tile), f32),
            pltpu.VMEM(tile, f32),
            pltpu.VMEM((nz, *tile), f32),
            pltpu.VMEM(tile, f32),
            dma((5,)),
            dma,
            dma((len(ROUTES[nz][3]) + 2,)),
            dma,
            dma((len(ROUTES[nz][3]) + 2,)),
        ]
        + [dma] * 12,
        compiler_params=pltpu.CompilerParams(collective_id=0, has_side_effects=True),
    )(queries, key_states, samples, query_gate_weight, key_gate_weight)
    return pl.pallas_call(
        finish,
        out_shape=(
            jax.ShapeDtypeStruct((8, 8), f32),
            jax.ShapeDtypeStruct((BLOCK, BLOCK), f32),
            jax.ShapeDtypeStruct((3 * BLOCK, BLOCK), f32),
        ),
        in_specs=[vmem] * 4,
        out_specs=(vmem,) * 3,
    )(*[pltpu.with_memory_space_constraint(a, pltpu.VMEM) for a in handed])


SEQ = ("yl", "z", "c")
KV = ("x", "yh")


def build(mesh, sizes):
    nz, nx, nyh = sizes
    torus = Mesh(mesh.devices.reshape(2, nz, 2, nx, nyh), (*SEQ, *KV))
    placed = (P(KV, SEQ, None), P(KV, SEQ, None), P(KV, SEQ), P(), P())
    return jax.shard_map(
        functools.partial(body, sizes),
        mesh=torus,
        in_specs=placed,
        out_specs=(P(KV, SEQ), P(), P()),
        check_vma=False,
    )


def solution(mesh):
    return build(mesh, (mesh.shape["seq"] // 4, mesh.shape["kv"] // 2, 2))
```

```python
import functools
import math

import jax
import jax.numpy as jnp
from jax import lax
from jax.experimental import pallas as pl
from jax.experimental.pallas import tpu as pltpu
from jax.sharding import Mesh
from jax.sharding import PartitionSpec as P

BLOCK = 128
MESH = pl.DeviceIdType.MESH
LOW = -1e30
highest = lax.Precision.HIGHEST
NN = (((1,), (0,)), ((), ()))
NT = (((1,), (1,)), ((), ()))
TN = (((0,), (0,)), ((), ()))
ROUTES = {
    4: ((1,), (1,), (), ((0, 1, 2, 3),)),
    8: ((1, 3), (1, -1), (1,), ((0, 1, 7, 3), (5, 4, 2, 6))),
    16: (
        (1, 2, 4),
        (4, 3, 2, 1, -1),
        (-3, -2, -1, 1),
        ((0, 1, 2, 15), (14, 4, 12, 5), (6, 7, 8, 9), (10, 11, 3, 13)),
    ),
}


def dot32(a, b, dims=NN):
    return lax.dot_general(a, b, dims, precision=highest, preferred_element_type=jnp.float32)


def partner(place, apart, size):
    if apart == 0:
        return place
    if size == 2:
        return 1 - place
    return (place + 1 - 2 * (place % 2), (place + 2) % 4, 3 - place)[apart - 1]


def kernel(
    sizes,
    q_hbm,
    k_hbm,
    samples_hbm,
    wq_hbm,
    wk_hbm,
    loss_ref,
    total_ref,
    wq_ref,
    wk_ref,
    q_ref,
    keys,
    samples_ref,
    pooled,
    queries,
    packed,
    returned,
    part,
    from_slice,
    slice_sum,
    from_z,
    z_sum,
    load_sem,
    query_send,
    query_recv,
    pool_send,
    pool_recv,
    keys_send,
    keys_recv,
    tile_send,
    tile_recv,
    back_send,
    back_recv,
    sum_send,
    sum_recv,
    z_send,
    z_recv,
    all_send,
    all_recv,
):
    nz, nx, nyh = sizes
    ny = 2 * nyh
    near_z, upper, lower, groups = ROUTES[nz]
    far = near_z[-1]
    z, yl, c = lax.axis_index("z"), lax.axis_index("yl"), lax.axis_index("c")
    x, yh = lax.axis_index("x"), lax.axis_index("yh")
    y = 2 * yh + yl
    def send(src, dst, send_sem, recv_sem, target):
        copy = pltpu.make_async_remote_copy(
            src_ref=src,
            dst_ref=dst,
            send_sem=send_sem,
            recv_sem=recv_sem,
            device_id=target,
            device_id_type=MESH,
        )
        copy.start()
        return copy

    def wait_for(ref, sem):
        pltpu.make_async_copy(ref, ref, sem).wait()

    def along_z(step):
        return {"z": (z + step + nz) % nz}

    def in_slice(i):
        return {"yl": partner(yl, i // 2, 2), "c": partner(c, i % 2, 2)}

    def along_xy(n):
        other = partner(y, n // 2 % ny, ny)
        return {
            "x": partner(x, n // (2 * ny), nx),
            "yh": other // 2,
            "yl": other % 2,
            "c": partner(c, n % 2, 2),
        }

    slice_size = 2 * nx * ny
    hops = (0, 1, 2, 1)
    others = sorted(
        range(1, slice_size), key=lambda n: -hops[n // (2 * ny)] - hops[n // 2 % ny]
    )
    touched = sorted({*near_z, *map(abs, upper), *map(abs, lower)}, reverse=True)
    near = [along_z(sign * d) for d in touched for sign in (1, -1)]
    near += [along_xy(n) for n in others]
    loads = [
        pltpu.make_async_copy(src, dst, load_sem.at[n])
        for n, (src, dst) in enumerate(
            (
                (samples_hbm, samples_ref),
                (q_hbm, q_ref),
                (k_hbm.at[0], keys.at[0]),
                (wq_hbm, wq_ref),
                (wk_hbm, wk_ref),
            )
        )
    ]
    for load in loads:
        load.start()

    barrier = pltpu.get_barrier_semaphore()
    for target in near:
        pl.semaphore_signal(barrier, inc=1, device_id=target, device_id_type=MESH)

    loads[2].wait()
    own = keys[0].astype(jnp.float32)
    blocks = (own[:BLOCK], own[BLOCK:])
    pooled[0, 0] = jnp.concatenate(
        [jnp.max(b, axis=0, keepdims=True) for b in blocks]
        + [jnp.min(b, axis=0, keepdims=True) for b in blocks]
        + [jnp.sum(b, axis=0, keepdims=True) * (1.0 / BLOCK) for b in blocks]
        + [jnp.zeros((2, own.shape[1]), jnp.float32)],
        axis=0,
    )

    loads[0].wait()
    shard = (yl * nz + z) * 2 + c
    local = (samples_ref[...] - shard * (2 * BLOCK)).astype(jnp.float32)
    spread = jnp.concatenate([jnp.broadcast_to(local[h : h + 1], (8, 8)) for h in range(8)], axis=0)
    lanes8 = lax.broadcasted_iota(jnp.int32, (64, 8), 1)
    rows8 = lax.broadcasted_iota(jnp.int32, (64, 8), 0) % 8
    column = jnp.sum(jnp.where(lanes8 == rows8, spread, 0.0), axis=1, keepdims=True)
    tokens = lax.broadcasted_iota(jnp.int32, (8, 2 * BLOCK), 1)
    query_rows, pooled_rows = [], []
    loads[1].wait()
    for h in range(8):
        place = column[8 * h : 8 * h + 8].astype(jnp.int32)
        chosen = jnp.where(tokens == place, 1.0, 0.0)
        block = jnp.where(tokens // BLOCK == place // BLOCK, 1.0, 0.0)
        both = lax.dot_general(
            jnp.concatenate([chosen, block], axis=0).astype(jnp.bfloat16),
            q_ref[h],
            NN,
            preferred_element_type=jnp.float32,
        )
        query_rows.append(both[:8])
        pooled_rows.append(both[8:] * (1.0 / BLOCK))
    queries[0] = jnp.concatenate(query_rows, axis=0).astype(jnp.bfloat16)

    pl.semaphore_wait(barrier, len(near))

    far_places = (far, nz - far)
    group_of = {at: g for g, group in enumerate(groups) for at in group}
    group_of.update({at: len(groups) + n for n, at in enumerate(far_places)})
    waits = [[at for at in group if at not in (0, *far_places)] for group in groups]

    def pass_pool(held, step):
        at = (held + step + nz) % nz
        send(
            pooled.at[0, held, :6],
            pooled.at[0, at, :6],
            pool_send,
            pool_recv.at[group_of[at]],
            along_z(step),
        )

    def pass_query(held, step):
        at = (held + step + nz) % nz
        send(
            queries.at[held],
            queries.at[at],
            query_send,
            query_recv.at[group_of[at]],
            along_z(step),
        )

    for d in reversed(near_z):
        for sign in (1, -1):
            pass_query(0, sign * d)
    for d in reversed(near_z):
        for sign in (1, -1):
            pass_pool(0, sign * d)
    for i in (2, 3, 1):
        send(keys.at[0], keys.at[i], keys_send, keys_recv, in_slice(i))
    pooled_rows = jnp.concatenate(pooled_rows + [jnp.zeros((64, BLOCK), jnp.float32)], axis=0)
    loads[3].wait()
    gate_rows = dot32(pooled_rows, wq_ref[...])
    pooled_columns = pooled_rows.T
    lanes = lax.broadcasted_iota(jnp.int32, (1, 256), 1)
    eye = lax.broadcasted_iota(jnp.int32, (64, 256), 0) == lax.broadcasted_iota(
        jnp.int32, (64, 256), 1
    )
    places = jnp.sum(jnp.where(eye, column, 0.0), axis=0, keepdims=True).astype(jnp.int32)
    places = jnp.where(lanes < 64, places, 2 * BLOCK - 1)

    for pass_on, kept, recv in (
        (pass_query, queries, query_recv),
        (pass_pool, pooled.at[0], pool_recv),
    ):
        for held, steps in zip(far_places, (upper, lower)):
            wait_for(kept.at[held] if kept is queries else kept.at[held, :6], recv.at[group_of[held]])
            for step in steps:
                pass_on(held, step)

    wait_for(keys.at[1:4], keys_recv)
    exponent = math.log2(math.e) / math.sqrt(BLOCK)
    first = lax.broadcasted_iota(jnp.int32, (8, BLOCK), 1) < 64

    def score(slots, waited):
        wait_for(queries.at[: len(waited)], query_recv.at[group_of[waited[0]]])
        rows = jnp.concatenate([queries[at] for at in slots], axis=0)
        tops, sums = [], []
        for i in range(4):
            scores = lax.dot_general(keys[i], rows, NT, preferred_element_type=jnp.float32)
            if i == 0 and slots[0] == 0:
                token = lax.broadcasted_iota(jnp.int32, scores.shape, 0)
                scores = jnp.where(token <= places, scores, LOW)
            for b in range(2):
                block_scores = scores[b * BLOCK : (b + 1) * BLOCK]
                highest_score = jnp.max(block_scores, axis=0, keepdims=True)
                weights = jnp.exp2((block_scores - highest_score) * exponent)
                tops.append(highest_score)
                sums.append(jnp.sum(weights, axis=0, keepdims=True))
        tops = jnp.concatenate(tops, axis=0)
        sums = jnp.concatenate(sums, axis=0)
        for pair in range(2):
            top = tops[:, pair * BLOCK : (pair + 1) * BLOCK]
            mass = sums[:, pair * BLOCK : (pair + 1) * BLOCK]
            packed[slots[2 * pair]] = jnp.where(first, top, pltpu.roll(mass, 64, 1))
            packed[slots[2 * pair + 1]] = jnp.where(first, pltpu.roll(top, 64, 1), mass)
        for at in slots:
            if at:
                back = nz - at
                send(packed.at[at], returned.at[back], back_send, back_recv, along_z(-at))

    def share_tiles(group, waited):
        wait_for(pooled.at[0, : len(waited), :6], pool_recv.at[group_of[waited[0]]])
        for at in group:
            for i in (2, 3, 1):
                send(
                    pooled.at[0, at, :6], pooled.at[i, at, :6], tile_send, tile_recv, in_slice(i)
                )

    for n, (group, waited) in enumerate(zip(groups, waits)):
        score(group, waited)
        if n < len(groups) - 2:
            share_tiles(group, waited)
    for group, waited in list(zip(groups, waits))[-2:]:
        share_tiles(group, waited)
    returned[0] = packed[0]
    loads[4].wait()
    wait_for(pooled.at[1:4, :, :6], tile_recv)

    nb = 8 * nz
    pooled_keys = jnp.concatenate(
        [
            jnp.concatenate([pooled[i, :, 2 * kind + b, :] for kind in range(3)], axis=1)
            for i in range(4)
            for b in range(2)
        ],
        axis=0,
    )
    gate_key = dot32(pooled_keys, wk_ref[...])
    gate_scale = 1.0 / math.sqrt(BLOCK)
    logits = dot32(gate_key, gate_rows, NT) * gate_scale
    order = lax.broadcasted_iota(jnp.int32, (nb, BLOCK), 0)
    lane = lax.broadcasted_iota(jnp.int32, (nb, BLOCK), 1)
    i_of = order // (2 * nz)
    b_of = order // nz % 2
    z_of = (z - order % nz + nz) % nz
    yl_of = (yl + i_of // 2) % 2
    c_of = (c + i_of % 2) % 2
    block_of = ((yl_of * nz + z_of) * 2 + c_of) * 2 + b_of
    own_block = 2 * shard + places[:, :BLOCK] // BLOCK
    allowed = block_of <= own_block
    logit_top = jnp.max(jnp.where(allowed, logits, LOW), axis=0, keepdims=True)
    gate_weights = jnp.where(allowed, jnp.exp(logits - logit_top), 0.0)
    gate_total = jnp.sum(gate_weights, axis=0, keepdims=True)
    log_total = logit_top + jnp.log(gate_total)
    gate = gate_weights / gate_total

    wait_for(returned.at[1:], back_recv)
    pairs = jnp.concatenate([returned[:, r, :] for r in range(8)], axis=0)
    sums = pltpu.roll(pairs, 64, 1)
    row_top = jnp.max(jnp.where(allowed, pairs, LOW), axis=0, keepdims=True)
    masses = jnp.where(allowed, sums * jnp.exp2((pairs - row_top) * exponent), 0.0)
    teacher = masses / jnp.sum(masses, axis=0, keepdims=True)
    losses = log_total - jnp.sum(jnp.where(allowed, teacher * logits, 0.0), axis=0, keepdims=True)
    delta = jnp.where(allowed & (lane < 64), (gate - teacher) * gate_scale, 0.0)

    block_query = dot32(pooled_columns, delta, NT)
    local_sum = dot32(block_query, pooled_keys)
    rows = BLOCK // slice_size
    for n in range(slice_size):
        for kind in range(3):
            part[n, kind] = local_sum[rows * n : rows * (n + 1), BLOCK * kind : BLOCK * (kind + 1)]

    def place_of(n):
        at = partner(x, n // (2 * ny), nx) * ny + partner(y, n // 2 % ny, ny)
        return 2 * at + partner(c, n % 2, 2)

    for n in others:
        send(part.at[place_of(n)], from_slice.at[n], sum_send, sum_recv, along_xy(n))
    head_of = lax.broadcasted_iota(jnp.int32, (8, BLOCK), 1) // 8
    head = lax.broadcasted_iota(jnp.int32, (8, BLOCK), 0)
    row_of = lax.broadcasted_iota(jnp.int32, (BLOCK, BLOCK), 0) % 8
    row = lax.broadcasted_iota(jnp.int32, (BLOCK, BLOCK), 1)
    by_head = jnp.where(head_of == head, jnp.broadcast_to(losses, (8, BLOCK)), 0.0)
    loss_ref[...] = dot32(by_head, jnp.where(row_of == row, 1.0, 0.0))[:, :8]
    total = part[place_of(0)]
    wait_for(from_slice.at[1:], sum_recv)
    for n in range(1, slice_size):
        total = total + from_slice[n]
    slice_sum[...] = total

    far_first = sorted(range(1, nz), key=lambda d: -min(d, nz - d))
    for d in far_first:
        send(slice_sum, from_z.at[z], z_send, z_recv, along_z(d))
    from_z[z] = total
    wait_for(from_z.at[1:], z_recv)
    total = from_z[0]
    for i in range(1, nz):
        total = total + from_z[i]

    z_sum[...] = total
    for n in others:
        send(z_sum, total_ref.at[place_of(0)], all_send, all_recv, along_xy(n))
    total_ref[place_of(0)] = total
    wait_for(queries.at[1:], query_send)
    wait_for(pooled.at[0, 1:, :6], pool_send)
    wait_for(keys.at[1:], keys_send)
    wait_for(packed.at[1:], back_send)
    wait_for(pooled.at[1:, :, :6], tile_send)
    wait_for(part.at[1:], sum_send)
    wait_for(from_z.at[1:], z_send)
    wait_for(from_slice.at[1:], all_send)
    wait_for(from_slice.at[1:], all_recv)


def finish(loss_ref, total_ref, wq_ref, wk_ref, row_loss_ref, query_grad_ref, key_grad_ref):
    total = jnp.concatenate(
        [
            jnp.concatenate([total_ref[n, kind] for n in range(total_ref.shape[0])], axis=0)
            for kind in range(3)
        ],
        axis=1,
    )
    query_grad_ref[...] = dot32(total, wk_ref[...])
    key_grad_ref[...] = dot32(total, wq_ref[...], TN)
    row_loss_ref[...] = loss_ref[...]


def body(sizes, queries, key_states, samples, query_gate_weight, key_gate_weight):
    nz, nx, nyh = sizes
    slice_size = 4 * nx * nyh
    tile = (3, BLOCK // slice_size, BLOCK)
    f32, bf16 = jnp.float32, jnp.bfloat16
    dma = pltpu.SemaphoreType.DMA
    vmem = pl.BlockSpec(memory_space=pltpu.VMEM)
    handed = pl.pallas_call(
        functools.partial(kernel, sizes),
        out_shape=(
            pltpu.VMEM((8, 8), f32),
            pltpu.VMEM((slice_size, *tile), f32),
            pltpu.VMEM((BLOCK, BLOCK), f32),
            pltpu.VMEM((3 * BLOCK, BLOCK), f32),
        ),
        in_specs=[pl.BlockSpec(memory_space=pl.ANY)] * 5,
        out_specs=(vmem,) * 4,
        scratch_shapes=[
            pltpu.VMEM((8, 2 * BLOCK, BLOCK), bf16),
            pltpu.VMEM((4, 2 * BLOCK, BLOCK), bf16),
            pltpu.VMEM((8, 8), jnp.int32),
            pltpu.VMEM((4, nz, 8, BLOCK), f32),
            pltpu.VMEM((nz, 64, BLOCK), bf16),
            pltpu.VMEM((nz, 8, BLOCK), f32),
            pltpu.VMEM((nz, 8, BLOCK), f32),
            pltpu.VMEM((slice_size, *tile), f32),
            pltpu.VMEM((slice_size, *tile), f32),
            pltpu.VMEM(tile, f32),
            pltpu.VMEM((nz, *tile), f32),
            pltpu.VMEM(tile, f32),
            dma((5,)),
            dma,
            dma((len(ROUTES[nz][3]) + 2,)),
            dma,
            dma((len(ROUTES[nz][3]) + 2,)),
        ]
        + [dma] * 12,
        compiler_params=pltpu.CompilerParams(collective_id=0, has_side_effects=True),
    )(queries, key_states, samples, query_gate_weight, key_gate_weight)
    return pl.pallas_call(
        finish,
        out_shape=(
            jax.ShapeDtypeStruct((8, 8), f32),
            jax.ShapeDtypeStruct((BLOCK, BLOCK), f32),
            jax.ShapeDtypeStruct((3 * BLOCK, BLOCK), f32),
        ),
        in_specs=[vmem] * 4,
        out_specs=(vmem,) * 3,
    )(*[pltpu.with_memory_space_constraint(a, pltpu.VMEM) for a in handed])


SEQ = ("yl", "z", "c")
KV = ("x", "yh")


def build(mesh, sizes):
    nz, nx, nyh = sizes
    torus = Mesh(mesh.devices.reshape(2, nz, 2, nx, nyh), (*SEQ, *KV))
    placed = (P(KV, SEQ, None), P(KV, SEQ, None), P(KV, SEQ), P(), P())
    return jax.shard_map(
        functools.partial(body, sizes),
        mesh=torus,
        in_specs=placed,
        out_specs=(P(KV, SEQ), P(), P()),
        check_vma=False,
    )


def solution(mesh):
    return build(mesh, (mesh.shape["seq"] // 4, mesh.shape["kv"] // 2, 2))
```

```python
import functools
import math

import jax
import jax.numpy as jnp
from jax import lax
from jax.experimental import pallas as pl
from jax.experimental.pallas import tpu as pltpu
from jax.sharding import Mesh
from jax.sharding import PartitionSpec as P

BLOCK = 128
MESH = pl.DeviceIdType.MESH
LOW = -1e30
highest = lax.Precision.HIGHEST
NN = (((1,), (0,)), ((), ()))
NT = (((1,), (1,)), ((), ()))
TN = (((0,), (0,)), ((), ()))
ROUTES = {
    4: ((1,), (1,), (), ((0, 1, 2, 3),)),
    8: ((1, 3), (1, -1), (1,), ((0, 1, 7, 3), (5, 4, 2, 6))),
    16: (
        (1, 2, 4),
        (4, 3, 2, 1, -1),
        (-3, -2, -1, 1),
        ((0, 1, 2, 15), (14, 4, 12, 5), (6, 7, 8, 9), (10, 11, 3, 13)),
    ),
}


def dot32(a, b, dims=NN):
    return lax.dot_general(a, b, dims, precision=highest, preferred_element_type=jnp.float32)


def partner(place, apart, size):
    if apart == 0:
        return place
    if size == 2:
        return 1 - place
    return (place + 1 - 2 * (place % 2), (place + 2) % 4, 3 - place)[apart - 1]


def kernel(
    sizes,
    q_hbm,
    k_hbm,
    samples_hbm,
    wq_hbm,
    wk_hbm,
    loss_ref,
    total_ref,
    wq_ref,
    wk_ref,
    q_ref,
    keys,
    samples_ref,
    pooled,
    queries,
    packed,
    returned,
    part,
    from_slice,
    slice_sum,
    from_z,
    z_sum,
    load_sem,
    query_send,
    query_recv,
    pool_send,
    pool_recv,
    keys_send,
    keys_recv,
    tile_send,
    tile_recv,
    back_send,
    back_recv,
    sum_send,
    sum_recv,
    z_send,
    z_recv,
    all_send,
    all_recv,
):
    nz, nx, nyh = sizes
    ny = 2 * nyh
    near_z, upper, lower, groups = ROUTES[nz]
    far = near_z[-1]
    z, yl, c = lax.axis_index("z"), lax.axis_index("yl"), lax.axis_index("c")
    x, yh = lax.axis_index("x"), lax.axis_index("yh")
    y = 2 * yh + yl
    def send(src, dst, send_sem, recv_sem, target):
        copy = pltpu.make_async_remote_copy(
            src_ref=src,
            dst_ref=dst,
            send_sem=send_sem,
            recv_sem=recv_sem,
            device_id=target,
            device_id_type=MESH,
        )
        copy.start()
        return copy

    def wait_for(ref, sem):
        pltpu.make_async_copy(ref, ref, sem).wait()

    def along_z(step):
        return {"z": (z + step + nz) % nz}

    def in_slice(i):
        return {"yl": partner(yl, i // 2, 2), "c": partner(c, i % 2, 2)}

    def along_xy(n):
        other = partner(y, n // 2 % ny, ny)
        return {
            "x": partner(x, n // (2 * ny), nx),
            "yh": other // 2,
            "yl": other % 2,
            "c": partner(c, n % 2, 2),
        }

    slice_size = 2 * nx * ny
    hops = (0, 1, 2, 1)
    others = sorted(
        range(1, slice_size), key=lambda n: -hops[n // (2 * ny)] - hops[n // 2 % ny]
    )
    touched = sorted({*near_z, *map(abs, upper), *map(abs, lower)}, reverse=True)
    near = [along_z(sign * d) for d in touched for sign in (1, -1)]
    near += [along_xy(n) for n in others]
    loads = [
        pltpu.make_async_copy(src, dst, load_sem.at[n])
        for n, (src, dst) in enumerate(
            (
                (samples_hbm, samples_ref),
                (q_hbm, q_ref),
                (k_hbm.at[0], keys.at[0]),
                (wq_hbm, wq_ref),
                (wk_hbm, wk_ref),
            )
        )
    ]
    for load in loads:
        load.start()

    barrier = pltpu.get_barrier_semaphore()
    for target in near:
        pl.semaphore_signal(barrier, inc=1, device_id=target, device_id_type=MESH)

    loads[2].wait()
    own = keys[0].astype(jnp.float32)
    blocks = (own[:BLOCK], own[BLOCK:])
    pooled[0, 0] = jnp.concatenate(
        [jnp.max(b, axis=0, keepdims=True) for b in blocks]
        + [jnp.min(b, axis=0, keepdims=True) for b in blocks]
        + [jnp.sum(b, axis=0, keepdims=True) * (1.0 / BLOCK) for b in blocks]
        + [jnp.zeros((2, own.shape[1]), jnp.float32)],
        axis=0,
    )

    loads[0].wait()
    shard = (yl * nz + z) * 2 + c
    local = (samples_ref[...] - shard * (2 * BLOCK)).astype(jnp.float32)
    spread = jnp.concatenate([jnp.broadcast_to(local[h : h + 1], (8, 8)) for h in range(8)], axis=0)
    lanes8 = lax.broadcasted_iota(jnp.int32, (64, 8), 1)
    rows8 = lax.broadcasted_iota(jnp.int32, (64, 8), 0) % 8
    column = jnp.sum(jnp.where(lanes8 == rows8, spread, 0.0), axis=1, keepdims=True)
    tokens = lax.broadcasted_iota(jnp.int32, (8, 2 * BLOCK), 1)
    query_rows, pooled_rows = [], []
    loads[1].wait()
    for h in range(8):
        place = column[8 * h : 8 * h + 8].astype(jnp.int32)
        chosen = jnp.where(tokens == place, 1.0, 0.0)
        block = jnp.where(tokens // BLOCK == place // BLOCK, 1.0, 0.0)
        both = lax.dot_general(
            jnp.concatenate([chosen, block], axis=0).astype(jnp.bfloat16),
            q_ref[h],
            NN,
            preferred_element_type=jnp.float32,
        )
        query_rows.append(both[:8])
        pooled_rows.append(both[8:] * (1.0 / BLOCK))
    queries[0] = jnp.concatenate(query_rows, axis=0).astype(jnp.bfloat16)

    pl.semaphore_wait(barrier, len(near))

    far_places = (far, nz - far)
    group_of = {at: g for g, group in enumerate(groups) for at in group}
    group_of.update({at: len(groups) + n for n, at in enumerate(far_places)})
    waits = [[at for at in group if at not in (0, *far_places)] for group in groups]

    def pass_pool(held, step):
        at = (held + step + nz) % nz
        send(
            pooled.at[0, held, :6],
            pooled.at[0, at, :6],
            pool_send,
            pool_recv.at[group_of[at]],
            along_z(step),
        )

    def pass_query(held, step):
        at = (held + step + nz) % nz
        send(
            queries.at[held],
            queries.at[at],
            query_send,
            query_recv.at[group_of[at]],
            along_z(step),
        )

    for d in reversed(near_z):
        for sign in (1, -1):
            pass_query(0, sign * d)
    for d in reversed(near_z):
        for sign in (1, -1):
            pass_pool(0, sign * d)
    for i in (2, 3, 1):
        send(keys.at[0], keys.at[i], keys_send, keys_recv, in_slice(i))
    pooled_rows = jnp.concatenate(pooled_rows + [jnp.zeros((64, BLOCK), jnp.float32)], axis=0)
    loads[3].wait()
    gate_rows = dot32(pooled_rows, wq_ref[...])
    pooled_columns = pooled_rows.T
    lanes = lax.broadcasted_iota(jnp.int32, (1, 256), 1)
    eye = lax.broadcasted_iota(jnp.int32, (64, 256), 0) == lax.broadcasted_iota(
        jnp.int32, (64, 256), 1
    )
    places = jnp.sum(jnp.where(eye, column, 0.0), axis=0, keepdims=True).astype(jnp.int32)
    places = jnp.where(lanes < 64, places, 2 * BLOCK - 1)

    for pass_on, kept, recv in (
        (pass_query, queries, query_recv),
        (pass_pool, pooled.at[0], pool_recv),
    ):
        for held, steps in zip(far_places, (upper, lower)):
            wait_for(kept.at[held] if kept is queries else kept.at[held, :6], recv.at[group_of[held]])
            for step in steps:
                pass_on(held, step)

    wait_for(keys.at[1:4], keys_recv)
    exponent = math.log2(math.e) / math.sqrt(BLOCK)
    first = lax.broadcasted_iota(jnp.int32, (8, BLOCK), 1) < 64

    def score(slots, waited):
        wait_for(queries.at[: len(waited)], query_recv.at[group_of[waited[0]]])
        rows = jnp.concatenate([queries[at] for at in slots], axis=0)
        tops, sums = [], []
        for i in range(4):
            scores = lax.dot_general(keys[i], rows, NT, preferred_element_type=jnp.float32)
            if i == 0 and slots[0] == 0:
                token = lax.broadcasted_iota(jnp.int32, scores.shape, 0)
                scores = jnp.where(token <= places, scores, LOW)
            for b in range(2):
                block_scores = scores[b * BLOCK : (b + 1) * BLOCK]
                highest_score = jnp.max(block_scores, axis=0, keepdims=True)
                weights = jnp.exp2((block_scores - highest_score) * exponent)
                tops.append(highest_score)
                sums.append(jnp.sum(weights, axis=0, keepdims=True))
        tops = jnp.concatenate(tops, axis=0)
        sums = jnp.concatenate(sums, axis=0)
        for pair in range(2):
            top = tops[:, pair * BLOCK : (pair + 1) * BLOCK]
            mass = sums[:, pair * BLOCK : (pair + 1) * BLOCK]
            packed[slots[2 * pair]] = jnp.where(first, top, pltpu.roll(mass, 64, 1))
            packed[slots[2 * pair + 1]] = jnp.where(first, pltpu.roll(top, 64, 1), mass)
        for at in slots:
            if at:
                back = nz - at
                send(packed.at[at], returned.at[back], back_send, back_recv, along_z(-at))

    def share_tiles(group, waited):
        wait_for(pooled.at[0, : len(waited), :6], pool_recv.at[group_of[waited[0]]])
        for at in group:
            for i in (2, 3, 1):
                send(
                    pooled.at[0, at, :6], pooled.at[i, at, :6], tile_send, tile_recv, in_slice(i)
                )

    for n, (group, waited) in enumerate(zip(groups, waits)):
        score(group, waited)
        if n < len(groups) - 2:
            share_tiles(group, waited)
    for group, waited in list(zip(groups, waits))[-2:]:
        share_tiles(group, waited)
    returned[0] = packed[0]
    loads[4].wait()
    wait_for(pooled.at[1:4, :, :6], tile_recv)

    nb = 8 * nz
    pooled_keys = jnp.concatenate(
        [
            jnp.concatenate([pooled[i, :, 2 * kind + b, :] for kind in range(3)], axis=1)
            for i in range(4)
            for b in range(2)
        ],
        axis=0,
    )
    gate_key = dot32(pooled_keys, wk_ref[...])
    gate_scale = 1.0 / math.sqrt(BLOCK)
    logits = dot32(gate_key, gate_rows, NT) * gate_scale
    order = lax.broadcasted_iota(jnp.int32, (nb, BLOCK), 0)
    lane = lax.broadcasted_iota(jnp.int32, (nb, BLOCK), 1)
    i_of = order // (2 * nz)
    b_of = order // nz % 2
    z_of = (z - order % nz + nz) % nz
    yl_of = (yl + i_of // 2) % 2
    c_of = (c + i_of % 2) % 2
    block_of = ((yl_of * nz + z_of) * 2 + c_of) * 2 + b_of
    own_block = 2 * shard + places[:, :BLOCK] // BLOCK
    allowed = block_of <= own_block
    logit_top = jnp.max(jnp.where(allowed, logits, LOW), axis=0, keepdims=True)
    gate_weights = jnp.where(allowed, jnp.exp(logits - logit_top), 0.0)
    gate_total = jnp.sum(gate_weights, axis=0, keepdims=True)
    log_total = logit_top + jnp.log(gate_total)
    gate = gate_weights / gate_total

    wait_for(returned.at[1:], back_recv)
    pairs = jnp.concatenate([returned[:, r, :] for r in range(8)], axis=0)
    sums = pltpu.roll(pairs, 64, 1)
    row_top = jnp.max(jnp.where(allowed, pairs, LOW), axis=0, keepdims=True)
    masses = jnp.where(allowed, sums * jnp.exp2((pairs - row_top) * exponent), 0.0)
    teacher = masses / jnp.sum(masses, axis=0, keepdims=True)
    losses = log_total - jnp.sum(jnp.where(allowed, teacher * logits, 0.0), axis=0, keepdims=True)
    delta = jnp.where(allowed & (lane < 64), (gate - teacher) * gate_scale, 0.0)

    block_query = dot32(pooled_columns, delta, NT)
    local_sum = dot32(block_query, pooled_keys)
    chunks = nx * ny
    rows = BLOCK // chunks
    for n in range(chunks):
        for kind in range(3):
            part[n, kind] = local_sum[rows * n : rows * (n + 1), BLOCK * kind : BLOCK * (kind + 1)]

    def place_of(n):
        return partner(x, n // (2 * ny), nx) * ny + partner(y, n // 2 % ny, ny)

    for core in (0, 1):

        @pl.when(c == core)
        def share():
            for n in others:
                if n % 2 != core:
                    send(part.at[place_of(n)], from_slice.at[n], sum_send, sum_recv, along_xy(n))

    head_of = lax.broadcasted_iota(jnp.int32, (8, BLOCK), 1) // 8
    head = lax.broadcasted_iota(jnp.int32, (8, BLOCK), 0)
    row_of = lax.broadcasted_iota(jnp.int32, (BLOCK, BLOCK), 0) % 8
    row = lax.broadcasted_iota(jnp.int32, (BLOCK, BLOCK), 1)
    by_head = jnp.where(head_of == head, jnp.broadcast_to(losses, (8, BLOCK)), 0.0)
    loss_ref[...] = dot32(by_head, jnp.where(row_of == row, 1.0, 0.0))[:, :8]
    far_first = sorted(range(1, nz), key=lambda d: -min(d, nz - d))

    @pl.when(c == 1)
    def own():
        wait_for(from_slice.at[1:], sum_recv)
        total = part[place_of(0)]
        for n in range(1, slice_size):
            total = total + from_slice[n]
        slice_sum[...] = total
        for d in far_first:
            send(slice_sum, from_z.at[z], z_send, z_recv, along_z(d))
        from_z[z] = total
        wait_for(from_z.at[1:], z_recv)
        total = from_z[0]
        for i in range(1, nz):
            total = total + from_z[i]
        z_sum[...] = total
        for n in others:
            send(z_sum, total_ref.at[place_of(0)], all_send, all_recv, along_xy(n))
        total_ref[place_of(0)] = total

    wait_for(queries.at[1:], query_send)
    wait_for(pooled.at[0, 1:, :6], pool_send)
    wait_for(keys.at[1:], keys_send)
    wait_for(packed.at[1:], back_send)
    wait_for(pooled.at[1:, :, :6], tile_send)

    @pl.when(c == 0)
    def end_core_0():
        wait_for(part, sum_send)
        wait_for(part, all_recv)

    @pl.when(c == 1)
    def end_core_1():
        wait_for(part.at[1:], sum_send)
        wait_for(from_z.at[1:], z_send)
        wait_for(from_slice.at[1:], all_send)
        wait_for(part.at[1:], all_recv)


def finish(loss_ref, total_ref, wq_ref, wk_ref, row_loss_ref, query_grad_ref, key_grad_ref):
    total = jnp.concatenate(
        [
            jnp.concatenate([total_ref[n, kind] for n in range(total_ref.shape[0])], axis=0)
            for kind in range(3)
        ],
        axis=1,
    )
    query_grad_ref[...] = dot32(total, wk_ref[...])
    key_grad_ref[...] = dot32(total, wq_ref[...], TN)
    row_loss_ref[...] = loss_ref[...]


def body(sizes, queries, key_states, samples, query_gate_weight, key_gate_weight):
    nz, nx, nyh = sizes
    slice_size = 4 * nx * nyh
    chunks = slice_size // 2
    tile = (3, BLOCK // chunks, BLOCK)
    f32, bf16 = jnp.float32, jnp.bfloat16
    dma = pltpu.SemaphoreType.DMA
    vmem = pl.BlockSpec(memory_space=pltpu.VMEM)
    handed = pl.pallas_call(
        functools.partial(kernel, sizes),
        out_shape=(
            pltpu.VMEM((8, 8), f32),
            pltpu.VMEM((chunks, *tile), f32),
            pltpu.VMEM((BLOCK, BLOCK), f32),
            pltpu.VMEM((3 * BLOCK, BLOCK), f32),
        ),
        in_specs=[pl.BlockSpec(memory_space=pl.ANY)] * 5,
        out_specs=(vmem,) * 4,
        scratch_shapes=[
            pltpu.VMEM((8, 2 * BLOCK, BLOCK), bf16),
            pltpu.VMEM((4, 2 * BLOCK, BLOCK), bf16),
            pltpu.VMEM((8, 8), jnp.int32),
            pltpu.VMEM((4, nz, 8, BLOCK), f32),
            pltpu.VMEM((nz, 64, BLOCK), bf16),
            pltpu.VMEM((nz, 8, BLOCK), f32),
            pltpu.VMEM((nz, 8, BLOCK), f32),
            pltpu.VMEM((chunks, *tile), f32),
            pltpu.VMEM((slice_size, *tile), f32),
            pltpu.VMEM(tile, f32),
            pltpu.VMEM((nz, *tile), f32),
            pltpu.VMEM(tile, f32),
            dma((5,)),
            dma,
            dma((len(ROUTES[nz][3]) + 2,)),
            dma,
            dma((len(ROUTES[nz][3]) + 2,)),
        ]
        + [dma] * 12,
        compiler_params=pltpu.CompilerParams(collective_id=0, has_side_effects=True),
    )(queries, key_states, samples, query_gate_weight, key_gate_weight)
    return pl.pallas_call(
        finish,
        out_shape=(
            jax.ShapeDtypeStruct((8, 8), f32),
            jax.ShapeDtypeStruct((BLOCK, BLOCK), f32),
            jax.ShapeDtypeStruct((3 * BLOCK, BLOCK), f32),
        ),
        in_specs=[vmem] * 4,
        out_specs=(vmem,) * 3,
    )(*[pltpu.with_memory_space_constraint(a, pltpu.VMEM) for a in handed])


SEQ = ("yl", "z", "c")
KV = ("x", "yh")


def build(mesh, sizes):
    nz, nx, nyh = sizes
    torus = Mesh(mesh.devices.reshape(2, nz, 2, nx, nyh), (*SEQ, *KV))
    placed = (P(KV, SEQ, None), P(KV, SEQ, None), P(KV, SEQ), P(), P())
    return jax.shard_map(
        functools.partial(body, sizes),
        mesh=torus,
        in_specs=placed,
        out_specs=(P(KV, SEQ), P(), P()),
        check_vma=False,
    )


def solution(mesh):
    return build(mesh, (mesh.shape["seq"] // 4, mesh.shape["kv"] // 2, 2))
```

```python
import functools
import math

import jax
import jax.numpy as jnp
from jax import lax
from jax.experimental import pallas as pl
from jax.experimental.pallas import tpu as pltpu
from jax.sharding import Mesh
from jax.sharding import PartitionSpec as P

BLOCK = 128
MESH = pl.DeviceIdType.MESH
LOW = -1e30
highest = lax.Precision.HIGHEST
NN = (((1,), (0,)), ((), ()))
NT = (((1,), (1,)), ((), ()))
TN = (((0,), (0,)), ((), ()))
ROUTES = {
    4: ((1,), (1,), (), ((0, 1, 2, 3),)),
    8: ((1, 3), (1, -1), (1,), ((0, 1, 7, 3), (5, 4, 2, 6))),
    16: (
        (1, 2, 4),
        (4, 3, 2, 1, -1),
        (-3, -2, -1, 1),
        ((0, 1, 2, 15), (14, 4, 12, 5), (6, 7, 8, 9), (10, 11, 3, 13)),
    ),
}


def dot32(a, b, dims=NN):
    return lax.dot_general(a, b, dims, precision=highest, preferred_element_type=jnp.float32)


def partner(place, apart, size):
    if apart == 0:
        return place
    if size == 2:
        return 1 - place
    return (place + 1 - 2 * (place % 2), (place + 2) % 4, 3 - place)[apart - 1]


def kernel(
    sizes,
    q_hbm,
    k_hbm,
    samples_hbm,
    wq_hbm,
    wk_hbm,
    loss_ref,
    total_ref,
    wq_ref,
    wk_ref,
    q_ref,
    keys,
    samples_ref,
    pooled,
    queries,
    for_other,
    tile_for_other,
    packed,
    returned,
    part,
    from_slice,
    slice_sum,
    from_z,
    z_sum,
    load_sem,
    for_other_recv,
    tile_for_other_recv,
    passed_send,
    tile_passed_send,
    query_send,
    query_recv,
    pool_send,
    pool_recv,
    keys_send,
    keys_recv,
    tile_send,
    tile_recv,
    back_send,
    back_recv,
    sum_send,
    sum_recv,
    z_send,
    z_recv,
    all_send,
    all_recv,
):
    nz, nx, nyh = sizes
    ny = 2 * nyh
    near_z, upper, lower, groups = ROUTES[nz]
    far = near_z[-1]
    z, yl, c = lax.axis_index("z"), lax.axis_index("yl"), lax.axis_index("c")
    x, yh = lax.axis_index("x"), lax.axis_index("yh")
    y = 2 * yh + yl
    def send(src, dst, send_sem, recv_sem, target):
        copy = pltpu.make_async_remote_copy(
            src_ref=src,
            dst_ref=dst,
            send_sem=send_sem,
            recv_sem=recv_sem,
            device_id=target,
            device_id_type=MESH,
        )
        copy.start()
        return copy

    def wait_for(ref, sem):
        pltpu.make_async_copy(ref, ref, sem).wait()

    def along_z(step):
        return {"z": (z + step + nz) % nz}

    def in_slice(i):
        return {"yl": partner(yl, i // 2, 2), "c": partner(c, i % 2, 2)}

    def along_xy(n):
        other = partner(y, n // 2 % ny, ny)
        return {
            "x": partner(x, n // (2 * ny), nx),
            "yh": other // 2,
            "yl": other % 2,
            "c": partner(c, n % 2, 2),
        }

    slice_size = 2 * nx * ny
    hops = (0, 1, 2, 1)
    others = sorted(
        range(1, slice_size), key=lambda n: -hops[n // (2 * ny)] - hops[n // 2 % ny]
    )
    touched = sorted({*near_z, *map(abs, upper), *map(abs, lower)}, reverse=True)
    near = [along_z(sign * d) for d in touched for sign in (1, -1)]
    near += [{**target, "c": 1 - c} for target in near]
    near += [along_xy(n) for n in others]
    loads = [
        pltpu.make_async_copy(src, dst, load_sem.at[n])
        for n, (src, dst) in enumerate(
            (
                (samples_hbm, samples_ref),
                (q_hbm, q_ref),
                (k_hbm.at[0], keys.at[0]),
                (wq_hbm, wq_ref),
                (wk_hbm, wk_ref),
            )
        )
    ]
    for load in loads:
        load.start()

    barrier = pltpu.get_barrier_semaphore()
    for target in near:
        pl.semaphore_signal(barrier, inc=1, device_id=target, device_id_type=MESH)

    loads[2].wait()
    own = keys[0].astype(jnp.float32)
    blocks = (own[:BLOCK], own[BLOCK:])
    pooled[0, 0] = jnp.concatenate(
        [jnp.max(b, axis=0, keepdims=True) for b in blocks]
        + [jnp.min(b, axis=0, keepdims=True) for b in blocks]
        + [jnp.sum(b, axis=0, keepdims=True) * (1.0 / BLOCK) for b in blocks]
        + [jnp.zeros((2, own.shape[1]), jnp.float32)],
        axis=0,
    )

    loads[0].wait()
    shard = (yl * nz + z) * 2 + c
    local = (samples_ref[...] - shard * (2 * BLOCK)).astype(jnp.float32)
    spread = jnp.concatenate([jnp.broadcast_to(local[h : h + 1], (8, 8)) for h in range(8)], axis=0)
    lanes8 = lax.broadcasted_iota(jnp.int32, (64, 8), 1)
    rows8 = lax.broadcasted_iota(jnp.int32, (64, 8), 0) % 8
    column = jnp.sum(jnp.where(lanes8 == rows8, spread, 0.0), axis=1, keepdims=True)
    tokens = lax.broadcasted_iota(jnp.int32, (8, 2 * BLOCK), 1)
    query_rows, pooled_rows = [], []
    loads[1].wait()
    for h in range(8):
        place = column[8 * h : 8 * h + 8].astype(jnp.int32)
        chosen = jnp.where(tokens == place, 1.0, 0.0)
        block = jnp.where(tokens // BLOCK == place // BLOCK, 1.0, 0.0)
        both = lax.dot_general(
            jnp.concatenate([chosen, block], axis=0).astype(jnp.bfloat16),
            q_ref[h],
            NN,
            preferred_element_type=jnp.float32,
        )
        query_rows.append(both[:8])
        pooled_rows.append(both[8:] * (1.0 / BLOCK))
    queries[0] = jnp.concatenate(query_rows, axis=0).astype(jnp.bfloat16)

    pl.semaphore_wait(barrier, len(near))

    far_places = (far, nz - far)
    group_of = {at: g for g, group in enumerate(groups) for at in group}
    group_of.update({at: len(groups) + n for n, at in enumerate(far_places)})
    waits = [[at for at in group if at not in (0, *far_places)] for group in groups]

    def pass_pool(held, step):
        at = (held + step + nz) % nz
        send(
            pooled.at[0, held, :6],
            pooled.at[0, at, :6],
            pool_send,
            pool_recv.at[group_of[at]],
            along_z(step),
        )

    def pass_query(held, step):
        at = (held + step + nz) % nz
        send(
            queries.at[held],
            queries.at[at],
            query_send,
            query_recv.at[group_of[at]],
            along_z(step),
        )

    @pl.when(c == 0)
    def start_core_0():
        for n, sign in enumerate((1, -1)):
            far_chip = {**along_z(sign * far), "c": 1}
            send(queries.at[0], for_other.at[n], query_send, for_other_recv.at[n], far_chip)
        for n, sign in enumerate((1, -1)):
            far_chip = {**along_z(sign * far), "c": 1}
            send(
                pooled.at[0, 0, :6],
                tile_for_other.at[n, :6],
                pool_send,
                tile_for_other_recv.at[n],
                far_chip,
            )

    @pl.when(c == 1)
    def start_core_1():
        for sign in (1, -1):
            pass_query(0, sign * far)
        for sign in (1, -1):
            pass_pool(0, sign * far)

    for d in reversed(near_z[:-1]):
        for sign in (1, -1):
            pass_query(0, sign * d)
    for d in reversed(near_z[:-1]):
        for sign in (1, -1):
            pass_pool(0, sign * d)
    for i in (2, 3, 1):
        send(keys.at[0], keys.at[i], keys_send, keys_recv, in_slice(i))
    pooled_rows = jnp.concatenate(pooled_rows + [jnp.zeros((64, BLOCK), jnp.float32)], axis=0)
    loads[3].wait()
    gate_rows = dot32(pooled_rows, wq_ref[...])
    pooled_columns = pooled_rows.T
    lanes = lax.broadcasted_iota(jnp.int32, (1, 256), 1)
    eye = lax.broadcasted_iota(jnp.int32, (64, 256), 0) == lax.broadcasted_iota(
        jnp.int32, (64, 256), 1
    )
    places = jnp.sum(jnp.where(eye, column, 0.0), axis=0, keepdims=True).astype(jnp.int32)
    places = jnp.where(lanes < 64, places, 2 * BLOCK - 1)

    @pl.when(c == 1)
    def relay():
        for n, (held, steps) in enumerate(zip(far_places, (upper, lower))):
            wait_for(queries.at[held], query_recv.at[group_of[held]])
            for step in steps:
                pass_query(held, step)
            wait_for(for_other.at[n], for_other_recv.at[n])
            for step in (*steps, 0):
                at = (held + step) % nz
                send(
                    for_other.at[n],
                    queries.at[at],
                    passed_send,
                    query_recv.at[group_of[at]],
                    {**along_z(step), "c": 0},
                )
        for n, (held, steps) in enumerate(zip(far_places, (upper, lower))):
            wait_for(pooled.at[0, held, :6], pool_recv.at[group_of[held]])
            for step in steps:
                pass_pool(held, step)
            wait_for(tile_for_other.at[n, :6], tile_for_other_recv.at[n])
            for step in (*steps, 0):
                at = (held + step) % nz
                send(
                    tile_for_other.at[n, :6],
                    pooled.at[0, at, :6],
                    tile_passed_send,
                    pool_recv.at[group_of[at]],
                    {**along_z(step), "c": 0},
                )

    wait_for(keys.at[1:4], keys_recv)
    exponent = math.log2(math.e) / math.sqrt(BLOCK)
    first = lax.broadcasted_iota(jnp.int32, (8, BLOCK), 1) < 64

    def score(slots, waited):
        wait_for(queries.at[: len(waited)], query_recv.at[group_of[waited[0]]])
        rows = jnp.concatenate([queries[at] for at in slots], axis=0)
        tops, sums = [], []
        for i in range(4):
            scores = lax.dot_general(keys[i], rows, NT, preferred_element_type=jnp.float32)
            if i == 0 and slots[0] == 0:
                token = lax.broadcasted_iota(jnp.int32, scores.shape, 0)
                scores = jnp.where(token <= places, scores, LOW)
            for b in range(2):
                block_scores = scores[b * BLOCK : (b + 1) * BLOCK]
                highest_score = jnp.max(block_scores, axis=0, keepdims=True)
                weights = jnp.exp2((block_scores - highest_score) * exponent)
                tops.append(highest_score)
                sums.append(jnp.sum(weights, axis=0, keepdims=True))
        tops = jnp.concatenate(tops, axis=0)
        sums = jnp.concatenate(sums, axis=0)
        for pair in range(2):
            top = tops[:, pair * BLOCK : (pair + 1) * BLOCK]
            mass = sums[:, pair * BLOCK : (pair + 1) * BLOCK]
            packed[slots[2 * pair]] = jnp.where(first, top, pltpu.roll(mass, 64, 1))
            packed[slots[2 * pair + 1]] = jnp.where(first, pltpu.roll(top, 64, 1), mass)
        for at in slots:
            if at:
                back = nz - at
                send(packed.at[at], returned.at[back], back_send, back_recv, along_z(-at))

    def await_far(group, kind):
        @pl.when(c == 0)
        def core_0():
            for held in far_places:
                if held in group:
                    if kind == "query":
                        wait_for(queries.at[held], query_recv.at[group_of[held]])
                    else:
                        wait_for(pooled.at[0, held, :6], pool_recv.at[group_of[held]])

    def share_tiles(group, waited):
        await_far(group, "pool")
        wait_for(pooled.at[0, : len(waited), :6], pool_recv.at[group_of[waited[0]]])
        for at in group:
            for i in (2, 3, 1):
                send(
                    pooled.at[0, at, :6], pooled.at[i, at, :6], tile_send, tile_recv, in_slice(i)
                )

    for n, (group, waited) in enumerate(zip(groups, waits)):
        await_far(group, "query")
        score(group, waited)
        if n < len(groups) - 2:
            share_tiles(group, waited)
    for group, waited in list(zip(groups, waits))[-2:]:
        share_tiles(group, waited)
    returned[0] = packed[0]
    loads[4].wait()
    wait_for(pooled.at[1:4, :, :6], tile_recv)

    nb = 8 * nz
    pooled_keys = jnp.concatenate(
        [
            jnp.concatenate([pooled[i, :, 2 * kind + b, :] for kind in range(3)], axis=1)
            for i in range(4)
            for b in range(2)
        ],
        axis=0,
    )
    gate_key = dot32(pooled_keys, wk_ref[...])
    gate_scale = 1.0 / math.sqrt(BLOCK)
    logits = dot32(gate_key, gate_rows, NT) * gate_scale
    order = lax.broadcasted_iota(jnp.int32, (nb, BLOCK), 0)
    lane = lax.broadcasted_iota(jnp.int32, (nb, BLOCK), 1)
    i_of = order // (2 * nz)
    b_of = order // nz % 2
    z_of = (z - order % nz + nz) % nz
    yl_of = (yl + i_of // 2) % 2
    c_of = (c + i_of % 2) % 2
    block_of = ((yl_of * nz + z_of) * 2 + c_of) * 2 + b_of
    own_block = 2 * shard + places[:, :BLOCK] // BLOCK
    allowed = block_of <= own_block
    logit_top = jnp.max(jnp.where(allowed, logits, LOW), axis=0, keepdims=True)
    gate_weights = jnp.where(allowed, jnp.exp(logits - logit_top), 0.0)
    gate_total = jnp.sum(gate_weights, axis=0, keepdims=True)
    log_total = logit_top + jnp.log(gate_total)
    gate = gate_weights / gate_total

    wait_for(returned.at[1:], back_recv)
    pairs = jnp.concatenate([returned[:, r, :] for r in range(8)], axis=0)
    sums = pltpu.roll(pairs, 64, 1)
    row_top = jnp.max(jnp.where(allowed, pairs, LOW), axis=0, keepdims=True)
    masses = jnp.where(allowed, sums * jnp.exp2((pairs - row_top) * exponent), 0.0)
    teacher = masses / jnp.sum(masses, axis=0, keepdims=True)
    losses = log_total - jnp.sum(jnp.where(allowed, teacher * logits, 0.0), axis=0, keepdims=True)
    delta = jnp.where(allowed & (lane < 64), (gate - teacher) * gate_scale, 0.0)

    block_query = dot32(pooled_columns, delta, NT)
    local_sum = dot32(block_query, pooled_keys)
    chunks = nx * ny
    rows = BLOCK // chunks
    for n in range(chunks):
        for kind in range(3):
            part[n, kind] = local_sum[rows * n : rows * (n + 1), BLOCK * kind : BLOCK * (kind + 1)]

    def place_of(n):
        return partner(x, n // (2 * ny), nx) * ny + partner(y, n // 2 % ny, ny)

    for core in (0, 1):

        @pl.when(c == core)
        def share():
            for n in others:
                if n % 2 != core:
                    send(part.at[place_of(n)], from_slice.at[n], sum_send, sum_recv, along_xy(n))

    head_of = lax.broadcasted_iota(jnp.int32, (8, BLOCK), 1) // 8
    head = lax.broadcasted_iota(jnp.int32, (8, BLOCK), 0)
    row_of = lax.broadcasted_iota(jnp.int32, (BLOCK, BLOCK), 0) % 8
    row = lax.broadcasted_iota(jnp.int32, (BLOCK, BLOCK), 1)
    by_head = jnp.where(head_of == head, jnp.broadcast_to(losses, (8, BLOCK)), 0.0)
    loss_ref[...] = dot32(by_head, jnp.where(row_of == row, 1.0, 0.0))[:, :8]
    far_first = sorted(range(1, nz), key=lambda d: -min(d, nz - d))

    @pl.when(c == 1)
    def own():
        wait_for(from_slice.at[1:], sum_recv)
        total = part[place_of(0)]
        for n in range(1, slice_size):
            total = total + from_slice[n]
        slice_sum[...] = total
        for d in far_first:
            send(slice_sum, from_z.at[z], z_send, z_recv, along_z(d))
        from_z[z] = total
        wait_for(from_z.at[1:], z_recv)
        total = from_z[0]
        for i in range(1, nz):
            total = total + from_z[i]
        z_sum[...] = total
        for n in others:
            send(z_sum, total_ref.at[place_of(0)], all_send, all_recv, along_xy(n))
        total_ref[place_of(0)] = total

    passed = 2 + len(upper) + len(lower)
    wait_for(keys.at[1:], keys_send)
    wait_for(packed.at[1:], back_send)
    wait_for(pooled.at[1:, :, :6], tile_send)

    @pl.when(c == 0)
    def end_core_0():
        wait_for(queries.at[: 2 * len(near_z)], query_send)
        wait_for(pooled.at[0, : 2 * len(near_z), :6], pool_send)
        wait_for(part, sum_send)
        wait_for(part, all_recv)

    @pl.when(c == 1)
    def end_core_1():
        wait_for(queries.at[1:], query_send)
        wait_for(pooled.at[0, 1:, :6], pool_send)
        wait_for(queries.at[:passed], passed_send)
        wait_for(pooled.at[0, :passed, :6], tile_passed_send)
        wait_for(part.at[1:], sum_send)
        wait_for(from_z.at[1:], z_send)
        wait_for(from_slice.at[1:], all_send)
        wait_for(part.at[1:], all_recv)


def finish(loss_ref, total_ref, wq_ref, wk_ref, row_loss_ref, query_grad_ref, key_grad_ref):
    total = jnp.concatenate(
        [
            jnp.concatenate([total_ref[n, kind] for n in range(total_ref.shape[0])], axis=0)
            for kind in range(3)
        ],
        axis=1,
    )
    query_grad_ref[...] = dot32(total, wk_ref[...])
    key_grad_ref[...] = dot32(total, wq_ref[...], TN)
    row_loss_ref[...] = loss_ref[...]


def body(sizes, queries, key_states, samples, query_gate_weight, key_gate_weight):
    nz, nx, nyh = sizes
    slice_size = 4 * nx * nyh
    chunks = slice_size // 2
    tile = (3, BLOCK // chunks, BLOCK)
    f32, bf16 = jnp.float32, jnp.bfloat16
    dma = pltpu.SemaphoreType.DMA
    vmem = pl.BlockSpec(memory_space=pltpu.VMEM)
    handed = pl.pallas_call(
        functools.partial(kernel, sizes),
        out_shape=(
            pltpu.VMEM((8, 8), f32),
            pltpu.VMEM((chunks, *tile), f32),
            pltpu.VMEM((BLOCK, BLOCK), f32),
            pltpu.VMEM((3 * BLOCK, BLOCK), f32),
        ),
        in_specs=[pl.BlockSpec(memory_space=pl.ANY)] * 5,
        out_specs=(vmem,) * 4,
        scratch_shapes=[
            pltpu.VMEM((8, 2 * BLOCK, BLOCK), bf16),
            pltpu.VMEM((4, 2 * BLOCK, BLOCK), bf16),
            pltpu.VMEM((8, 8), jnp.int32),
            pltpu.VMEM((4, nz, 8, BLOCK), f32),
            pltpu.VMEM((nz, 64, BLOCK), bf16),
            pltpu.VMEM((2, 64, BLOCK), bf16),
            pltpu.VMEM((2, 8, BLOCK), f32),
            pltpu.VMEM((nz, 8, BLOCK), f32),
            pltpu.VMEM((nz, 8, BLOCK), f32),
            pltpu.VMEM((chunks, *tile), f32),
            pltpu.VMEM((slice_size, *tile), f32),
            pltpu.VMEM(tile, f32),
            pltpu.VMEM((nz, *tile), f32),
            pltpu.VMEM(tile, f32),
            dma((5,)),
            dma((2,)),
            dma((2,)),
            dma,
            dma,
            dma,
            dma((len(ROUTES[nz][3]) + 2,)),
            dma,
            dma((len(ROUTES[nz][3]) + 2,)),
        ]
        + [dma] * 12,
        compiler_params=pltpu.CompilerParams(collective_id=0, has_side_effects=True),
    )(queries, key_states, samples, query_gate_weight, key_gate_weight)
    return pl.pallas_call(
        finish,
        out_shape=(
            jax.ShapeDtypeStruct((8, 8), f32),
            jax.ShapeDtypeStruct((BLOCK, BLOCK), f32),
            jax.ShapeDtypeStruct((3 * BLOCK, BLOCK), f32),
        ),
        in_specs=[vmem] * 4,
        out_specs=(vmem,) * 3,
    )(*[pltpu.with_memory_space_constraint(a, pltpu.VMEM) for a in handed])


SEQ = ("yl", "z", "c")
KV = ("x", "yh")


def build(mesh, sizes):
    nz, nx, nyh = sizes
    torus = Mesh(mesh.devices.reshape(2, nz, 2, nx, nyh), (*SEQ, *KV))
    placed = (P(KV, SEQ, None), P(KV, SEQ, None), P(KV, SEQ), P(), P())
    return jax.shard_map(
        functools.partial(body, sizes),
        mesh=torus,
        in_specs=placed,
        out_specs=(P(KV, SEQ), P(), P()),
        check_vma=False,
    )


def solution(mesh):
    return build(mesh, (mesh.shape["seq"] // 4, mesh.shape["kv"] // 2, 2))
```

```python
import functools
import math

import jax
import jax.numpy as jnp
from jax import lax
from jax.experimental import pallas as pl
from jax.experimental.pallas import tpu as pltpu
from jax.sharding import Mesh
from jax.sharding import PartitionSpec as P

BLOCK = 128
MESH = pl.DeviceIdType.MESH
LOW = -1e30
highest = lax.Precision.HIGHEST
NN = (((1,), (0,)), ((), ()))
NT = (((1,), (1,)), ((), ()))
TN = (((0,), (0,)), ((), ()))
ROUTES = {
    4: ((1,), (1,), (), ((0, 1, 2, 3),)),
    8: ((1, 3), (1, -1), (1,), ((0, 1, 7, 3), (5, 4, 2, 6))),
    16: (
        (1, 2, 4),
        (4, 3, 2, 1, -1),
        (-3, -2, -1, 1),
        ((0, 1, 2, 15), (14, 4, 12, 5), (6, 7, 8, 9), (10, 11, 3, 13)),
    ),
}


def dot32(a, b, dims=NN):
    return lax.dot_general(a, b, dims, precision=highest, preferred_element_type=jnp.float32)


def partner(place, apart, size):
    if apart == 0:
        return place
    if size == 2:
        return 1 - place
    return (place + 1 - 2 * (place % 2), (place + 2) % 4, 3 - place)[apart - 1]


def kernel(
    sizes,
    q_hbm,
    k_hbm,
    samples_hbm,
    wq_hbm,
    wk_hbm,
    loss_ref,
    total_ref,
    wq_ref,
    wk_ref,
    q_ref,
    keys,
    samples_ref,
    pooled,
    queries,
    packed,
    returned,
    part,
    from_slice,
    slice_sum,
    from_z,
    z_sum,
    load_sem,
    query_send,
    query_recv,
    pool_send,
    pool_recv,
    keys_send,
    keys_recv,
    tile_send,
    tile_recv,
    back_send,
    back_recv,
    sum_send,
    sum_recv,
    z_send,
    z_recv,
    all_send,
    all_recv,
):
    nz, nx, nyh = sizes
    ny = 2 * nyh
    near_z, upper, lower, groups = ROUTES[nz]
    far = near_z[-1]
    z, yl, c = lax.axis_index("z"), lax.axis_index("yl"), lax.axis_index("c")
    x, yh = lax.axis_index("x"), lax.axis_index("yh")
    y = 2 * yh + yl
    def send(src, dst, send_sem, recv_sem, target):
        copy = pltpu.make_async_remote_copy(
            src_ref=src,
            dst_ref=dst,
            send_sem=send_sem,
            recv_sem=recv_sem,
            device_id=target,
            device_id_type=MESH,
        )
        copy.start()
        return copy

    def wait_for(ref, sem):
        pltpu.make_async_copy(ref, ref, sem).wait()

    def along_z(step):
        return {"z": (z + step + nz) % nz}

    def in_slice(i):
        return {"yl": partner(yl, i // 2, 2), "c": partner(c, i % 2, 2)}

    def along_xy(n):
        other = partner(y, n // 2 % ny, ny)
        return {
            "x": partner(x, n // (2 * ny), nx),
            "yh": other // 2,
            "yl": other % 2,
            "c": partner(c, n % 2, 2),
        }

    slice_size = 2 * nx * ny
    hops = (0, 1, 2, 1)
    others = sorted(
        range(1, slice_size), key=lambda n: -hops[n // (2 * ny)] - hops[n // 2 % ny]
    )
    touched = sorted({*near_z, *map(abs, upper), *map(abs, lower)}, reverse=True)
    near = [along_z(sign * d) for d in touched for sign in (1, -1)]
    near += [along_xy(n) for n in others]
    loads = [
        pltpu.make_async_copy(src, dst, load_sem.at[n])
        for n, (src, dst) in enumerate(
            (
                (samples_hbm, samples_ref),
                (q_hbm, q_ref),
                (k_hbm.at[0], keys.at[0]),
                (wq_hbm, wq_ref),
                (wk_hbm, wk_ref),
            )
        )
    ]
    for load in loads:
        load.start()

    barrier = pltpu.get_barrier_semaphore()
    for target in near:
        pl.semaphore_signal(barrier, inc=1, device_id=target, device_id_type=MESH)

    loads[2].wait()
    own = keys[0].astype(jnp.float32)
    blocks = (own[:BLOCK], own[BLOCK:])
    pooled[0, 0] = jnp.concatenate(
        [jnp.max(b, axis=0, keepdims=True) for b in blocks]
        + [jnp.min(b, axis=0, keepdims=True) for b in blocks]
        + [jnp.sum(b, axis=0, keepdims=True) * (1.0 / BLOCK) for b in blocks]
        + [jnp.zeros((2, own.shape[1]), jnp.float32)],
        axis=0,
    )

    loads[0].wait()
    shard = (yl * nz + z) * 2 + c
    local = (samples_ref[...] - shard * (2 * BLOCK)).astype(jnp.float32)
    spread = jnp.concatenate([jnp.broadcast_to(local[h : h + 1], (8, 8)) for h in range(8)], axis=0)
    lanes8 = lax.broadcasted_iota(jnp.int32, (64, 8), 1)
    rows8 = lax.broadcasted_iota(jnp.int32, (64, 8), 0) % 8
    column = jnp.sum(jnp.where(lanes8 == rows8, spread, 0.0), axis=1, keepdims=True)
    tokens = lax.broadcasted_iota(jnp.int32, (8, 2 * BLOCK), 1)
    query_rows, pooled_rows = [], []
    loads[1].wait()
    for h in range(8):
        place = column[8 * h : 8 * h + 8].astype(jnp.int32)
        chosen = jnp.where(tokens == place, 1.0, 0.0)
        block = jnp.where(tokens // BLOCK == place // BLOCK, 1.0, 0.0)
        both = lax.dot_general(
            jnp.concatenate([chosen, block], axis=0).astype(jnp.bfloat16),
            q_ref[h],
            NN,
            preferred_element_type=jnp.float32,
        )
        query_rows.append(both[:8])
        pooled_rows.append(both[8:] * (1.0 / BLOCK))
    queries[0] = jnp.concatenate(query_rows, axis=0).astype(jnp.bfloat16)

    pl.semaphore_wait(barrier, len(near))

    far_places = (far, nz - far)
    group_of = {at: g for g, group in enumerate(groups) for at in group}
    group_of.update({at: len(groups) + n for n, at in enumerate(far_places)})
    waits = [[at for at in group if at not in (0, *far_places)] for group in groups]

    def pass_pool(held, step):
        at = (held + step + nz) % nz
        send(
            pooled.at[0, held, :6],
            pooled.at[0, at, :6],
            pool_send,
            pool_recv.at[group_of[at]],
            along_z(step),
        )

    def pass_query(held, step):
        at = (held + step + nz) % nz
        send(
            queries.at[held],
            queries.at[at],
            query_send,
            query_recv.at[group_of[at]],
            along_z(step),
        )

    for d in reversed(near_z):
        for sign in (1, -1):
            pass_query(0, sign * d)
    for d in reversed(near_z):
        for sign in (1, -1):
            pass_pool(0, sign * d)
    for i in (2, 3, 1):
        send(keys.at[0], keys.at[i], keys_send, keys_recv, in_slice(i))
    pooled_rows = jnp.concatenate(pooled_rows + [jnp.zeros((64, BLOCK), jnp.float32)], axis=0)
    loads[3].wait()
    gate_rows = dot32(pooled_rows, wq_ref[...])
    pooled_columns = pooled_rows.T
    lanes = lax.broadcasted_iota(jnp.int32, (1, 256), 1)
    eye = lax.broadcasted_iota(jnp.int32, (64, 256), 0) == lax.broadcasted_iota(
        jnp.int32, (64, 256), 1
    )
    places = jnp.sum(jnp.where(eye, column, 0.0), axis=0, keepdims=True).astype(jnp.int32)
    places = jnp.where(lanes < 64, places, 2 * BLOCK - 1)

    for pass_on, kept, recv in (
        (pass_query, queries, query_recv),
        (pass_pool, pooled.at[0], pool_recv),
    ):
        for held, steps in zip(far_places, (upper, lower)):
            wait_for(kept.at[held] if kept is queries else kept.at[held, :6], recv.at[group_of[held]])
            for step in steps:
                pass_on(held, step)

    wait_for(keys.at[1:4], keys_recv)
    exponent = math.log2(math.e) / math.sqrt(BLOCK)
    first = lax.broadcasted_iota(jnp.int32, (8, BLOCK), 1) < 64

    def score(slots, waited):
        wait_for(queries.at[: len(waited)], query_recv.at[group_of[waited[0]]])
        rows = jnp.concatenate([queries[at] for at in slots], axis=0)
        tops, sums = [], []
        for i in range(4):
            scores = lax.dot_general(keys[i], rows, NT, preferred_element_type=jnp.float32)
            if i == 0 and slots[0] == 0:
                token = lax.broadcasted_iota(jnp.int32, scores.shape, 0)
                scores = jnp.where(token <= places, scores, LOW)
            for b in range(2):
                block_scores = scores[b * BLOCK : (b + 1) * BLOCK]
                highest_score = jnp.max(block_scores, axis=0, keepdims=True)
                weights = jnp.exp2((block_scores - highest_score) * exponent)
                tops.append(highest_score)
                sums.append(jnp.sum(weights, axis=0, keepdims=True))
        tops = jnp.concatenate(tops, axis=0)
        sums = jnp.concatenate(sums, axis=0)
        for pair in range(2):
            top = tops[:, pair * BLOCK : (pair + 1) * BLOCK]
            mass = sums[:, pair * BLOCK : (pair + 1) * BLOCK]
            packed[slots[2 * pair]] = jnp.where(first, top, pltpu.roll(mass, 64, 1))
            packed[slots[2 * pair + 1]] = jnp.where(first, pltpu.roll(top, 64, 1), mass)
        for at in slots:
            if at:
                back = nz - at
                send(packed.at[at], returned.at[back], back_send, back_recv, along_z(-at))

    def share_tiles(group, waited):
        wait_for(pooled.at[0, : len(waited), :6], pool_recv.at[group_of[waited[0]]])
        for at in group:
            for i in (2, 3, 1):
                send(
                    pooled.at[0, at, :6], pooled.at[i, at, :6], tile_send, tile_recv, in_slice(i)
                )

    for n, (group, waited) in enumerate(zip(groups, waits)):
        score(group, waited)
        if n < 1:
            share_tiles(group, waited)
    for group, waited in list(zip(groups, waits))[1:]:
        share_tiles(group, waited)
    returned[0] = packed[0]
    loads[4].wait()
    wait_for(pooled.at[1:4, :, :6], tile_recv)

    nb = 8 * nz
    pooled_keys = jnp.concatenate(
        [
            jnp.concatenate([pooled[i, :, 2 * kind + b, :] for kind in range(3)], axis=1)
            for i in range(4)
            for b in range(2)
        ],
        axis=0,
    )
    gate_key = dot32(pooled_keys, wk_ref[...])
    gate_scale = 1.0 / math.sqrt(BLOCK)
    logits = dot32(gate_key, gate_rows, NT) * gate_scale
    order = lax.broadcasted_iota(jnp.int32, (nb, BLOCK), 0)
    lane = lax.broadcasted_iota(jnp.int32, (nb, BLOCK), 1)
    i_of = order // (2 * nz)
    b_of = order // nz % 2
    z_of = (z - order % nz + nz) % nz
    yl_of = (yl + i_of // 2) % 2
    c_of = (c + i_of % 2) % 2
    block_of = ((yl_of * nz + z_of) * 2 + c_of) * 2 + b_of
    own_block = 2 * shard + places[:, :BLOCK] // BLOCK
    allowed = block_of <= own_block
    logit_top = jnp.max(jnp.where(allowed, logits, LOW), axis=0, keepdims=True)
    gate_weights = jnp.where(allowed, jnp.exp(logits - logit_top), 0.0)
    gate_total = jnp.sum(gate_weights, axis=0, keepdims=True)
    log_total = logit_top + jnp.log(gate_total)
    gate = gate_weights / gate_total

    wait_for(returned.at[1:], back_recv)
    pairs = jnp.concatenate([returned[:, r, :] for r in range(8)], axis=0)
    sums = pltpu.roll(pairs, 64, 1)
    row_top = jnp.max(jnp.where(allowed, pairs, LOW), axis=0, keepdims=True)
    masses = jnp.where(allowed, sums * jnp.exp2((pairs - row_top) * exponent), 0.0)
    teacher = masses / jnp.sum(masses, axis=0, keepdims=True)
    losses = log_total - jnp.sum(jnp.where(allowed, teacher * logits, 0.0), axis=0, keepdims=True)
    delta = jnp.where(allowed & (lane < 64), (gate - teacher) * gate_scale, 0.0)

    block_query = dot32(pooled_columns, delta, NT)
    local_sum = dot32(block_query, pooled_keys)
    chunks = nx * ny
    rows = BLOCK // chunks
    for n in range(chunks):
        for kind in range(3):
            part[n, kind] = local_sum[rows * n : rows * (n + 1), BLOCK * kind : BLOCK * (kind + 1)]

    def place_of(n):
        return partner(x, n // (2 * ny), nx) * ny + partner(y, n // 2 % ny, ny)

    for core in (0, 1):

        @pl.when(c == core)
        def share():
            for n in others:
                if n % 2 != core:
                    send(part.at[place_of(n)], from_slice.at[n], sum_send, sum_recv, along_xy(n))

    head_of = lax.broadcasted_iota(jnp.int32, (8, BLOCK), 1) // 8
    head = lax.broadcasted_iota(jnp.int32, (8, BLOCK), 0)
    row_of = lax.broadcasted_iota(jnp.int32, (BLOCK, BLOCK), 0) % 8
    row = lax.broadcasted_iota(jnp.int32, (BLOCK, BLOCK), 1)
    by_head = jnp.where(head_of == head, jnp.broadcast_to(losses, (8, BLOCK)), 0.0)
    loss_ref[...] = dot32(by_head, jnp.where(row_of == row, 1.0, 0.0))[:, :8]
    far_first = sorted(range(1, nz), key=lambda d: -min(d, nz - d))

    @pl.when(c == 1)
    def own():
        wait_for(from_slice.at[1:], sum_recv)
        total = part[place_of(0)]
        for n in range(1, slice_size):
            total = total + from_slice[n]
        slice_sum[...] = total
        for d in far_first:
            send(slice_sum, from_z.at[z], z_send, z_recv, along_z(d))
        from_z[z] = total
        wait_for(from_z.at[1:], z_recv)
        total = from_z[0]
        for i in range(1, nz):
            total = total + from_z[i]
        z_sum[...] = total
        for n in others:
            send(z_sum, total_ref.at[place_of(0)], all_send, all_recv, along_xy(n))
        total_ref[place_of(0)] = total

    wait_for(queries.at[1:], query_send)
    wait_for(pooled.at[0, 1:, :6], pool_send)
    wait_for(keys.at[1:], keys_send)
    wait_for(packed.at[1:], back_send)
    wait_for(pooled.at[1:, :, :6], tile_send)

    @pl.when(c == 0)
    def end_core_0():
        wait_for(part, sum_send)
        wait_for(part, all_recv)

    @pl.when(c == 1)
    def end_core_1():
        wait_for(part.at[1:], sum_send)
        wait_for(from_z.at[1:], z_send)
        wait_for(from_slice.at[1:], all_send)
        wait_for(part.at[1:], all_recv)


def finish(loss_ref, total_ref, wq_ref, wk_ref, row_loss_ref, query_grad_ref, key_grad_ref):
    total = jnp.concatenate(
        [
            jnp.concatenate([total_ref[n, kind] for n in range(total_ref.shape[0])], axis=0)
            for kind in range(3)
        ],
        axis=1,
    )
    query_grad_ref[...] = dot32(total, wk_ref[...])
    key_grad_ref[...] = dot32(total, wq_ref[...], TN)
    row_loss_ref[...] = loss_ref[...]


def body(sizes, queries, key_states, samples, query_gate_weight, key_gate_weight):
    nz, nx, nyh = sizes
    slice_size = 4 * nx * nyh
    chunks = slice_size // 2
    tile = (3, BLOCK // chunks, BLOCK)
    f32, bf16 = jnp.float32, jnp.bfloat16
    dma = pltpu.SemaphoreType.DMA
    vmem = pl.BlockSpec(memory_space=pltpu.VMEM)
    handed = pl.pallas_call(
        functools.partial(kernel, sizes),
        out_shape=(
            pltpu.VMEM((8, 8), f32),
            pltpu.VMEM((chunks, *tile), f32),
            pltpu.VMEM((BLOCK, BLOCK), f32),
            pltpu.VMEM((3 * BLOCK, BLOCK), f32),
        ),
        in_specs=[pl.BlockSpec(memory_space=pl.ANY)] * 5,
        out_specs=(vmem,) * 4,
        scratch_shapes=[
            pltpu.VMEM((8, 2 * BLOCK, BLOCK), bf16),
            pltpu.VMEM((4, 2 * BLOCK, BLOCK), bf16),
            pltpu.VMEM((8, 8), jnp.int32),
            pltpu.VMEM((4, nz, 8, BLOCK), f32),
            pltpu.VMEM((nz, 64, BLOCK), bf16),
            pltpu.VMEM((nz, 8, BLOCK), f32),
            pltpu.VMEM((nz, 8, BLOCK), f32),
            pltpu.VMEM((chunks, *tile), f32),
            pltpu.VMEM((slice_size, *tile), f32),
            pltpu.VMEM(tile, f32),
            pltpu.VMEM((nz, *tile), f32),
            pltpu.VMEM(tile, f32),
            dma((5,)),
            dma,
            dma((len(ROUTES[nz][3]) + 2,)),
            dma,
            dma((len(ROUTES[nz][3]) + 2,)),
        ]
        + [dma] * 12,
        compiler_params=pltpu.CompilerParams(collective_id=0, has_side_effects=True),
    )(queries, key_states, samples, query_gate_weight, key_gate_weight)
    return pl.pallas_call(
        finish,
        out_shape=(
            jax.ShapeDtypeStruct((8, 8), f32),
            jax.ShapeDtypeStruct((BLOCK, BLOCK), f32),
            jax.ShapeDtypeStruct((3 * BLOCK, BLOCK), f32),
        ),
        in_specs=[vmem] * 4,
        out_specs=(vmem,) * 3,
    )(*[pltpu.with_memory_space_constraint(a, pltpu.VMEM) for a in handed])


SEQ = ("yl", "z", "c")
KV = ("x", "yh")


def build(mesh, sizes):
    nz, nx, nyh = sizes
    torus = Mesh(mesh.devices.reshape(2, nz, 2, nx, nyh), (*SEQ, *KV))
    placed = (P(KV, SEQ, None), P(KV, SEQ, None), P(KV, SEQ), P(), P())
    return jax.shard_map(
        functools.partial(body, sizes),
        mesh=torus,
        in_specs=placed,
        out_specs=(P(KV, SEQ), P(), P()),
        check_vma=False,
    )


def solution(mesh):
    return build(mesh, (mesh.shape["seq"] // 4, mesh.shape["kv"] // 2, 2))
```

```python
import functools
import math

import jax
import jax.numpy as jnp
from jax import lax
from jax.experimental import pallas as pl
from jax.experimental.pallas import tpu as pltpu
from jax.sharding import Mesh
from jax.sharding import PartitionSpec as P

BLOCK = 128
MESH = pl.DeviceIdType.MESH
LOW = -1e30
highest = lax.Precision.HIGHEST
NN = (((1,), (0,)), ((), ()))
NT = (((1,), (1,)), ((), ()))
TN = (((0,), (0,)), ((), ()))
ROUTES = {
    4: ((1,), (1,), (), ((0, 1, 2, 3),)),
    8: ((1, 3), (1, -1), (1,), ((0, 1, 7, 3), (5, 4, 2, 6))),
    16: (
        (1, 2, 4),
        (4, 3, 2, 1, -1),
        (-3, -2, -1, 1),
        ((0, 1, 2, 15), (14, 4), (12, 3, 13, 5), (6, 7, 8, 9), (10, 11)),
    ),
}


def dot32(a, b, dims=NN):
    return lax.dot_general(a, b, dims, precision=highest, preferred_element_type=jnp.float32)


def partner(place, apart, size):
    if apart == 0:
        return place
    if size == 2:
        return 1 - place
    return (place + 1 - 2 * (place % 2), (place + 2) % 4, 3 - place)[apart - 1]


def kernel(
    sizes,
    q_hbm,
    k_hbm,
    samples_hbm,
    wq_hbm,
    wk_hbm,
    loss_ref,
    total_ref,
    wq_ref,
    wk_ref,
    q_ref,
    keys,
    samples_ref,
    pooled,
    queries,
    packed,
    returned,
    part,
    from_slice,
    slice_sum,
    from_z,
    z_sum,
    load_sem,
    query_send,
    query_recv,
    pool_send,
    pool_recv,
    keys_send,
    keys_recv,
    tile_send,
    tile_recv,
    back_send,
    back_recv,
    sum_send,
    sum_recv,
    z_send,
    z_recv,
    all_send,
    all_recv,
):
    nz, nx, nyh = sizes
    ny = 2 * nyh
    near_z, upper, lower, groups = ROUTES[nz]
    far = near_z[-1]
    z, yl, c = lax.axis_index("z"), lax.axis_index("yl"), lax.axis_index("c")
    x, yh = lax.axis_index("x"), lax.axis_index("yh")
    y = 2 * yh + yl
    def send(src, dst, send_sem, recv_sem, target):
        copy = pltpu.make_async_remote_copy(
            src_ref=src,
            dst_ref=dst,
            send_sem=send_sem,
            recv_sem=recv_sem,
            device_id=target,
            device_id_type=MESH,
        )
        copy.start()
        return copy

    def wait_for(ref, sem):
        pltpu.make_async_copy(ref, ref, sem).wait()

    def along_z(step):
        return {"z": (z + step + nz) % nz}

    def in_slice(i):
        return {"yl": partner(yl, i // 2, 2), "c": partner(c, i % 2, 2)}

    def along_xy(n):
        other = partner(y, n // 2 % ny, ny)
        return {
            "x": partner(x, n // (2 * ny), nx),
            "yh": other // 2,
            "yl": other % 2,
            "c": partner(c, n % 2, 2),
        }

    slice_size = 2 * nx * ny
    hops = (0, 1, 2, 1)
    others = sorted(
        range(1, slice_size), key=lambda n: -hops[n // (2 * ny)] - hops[n // 2 % ny]
    )
    touched = sorted({*near_z, *map(abs, upper), *map(abs, lower)}, reverse=True)
    near = [along_z(sign * d) for d in touched for sign in (1, -1)]
    near += [along_xy(n) for n in others]
    loads = [
        pltpu.make_async_copy(src, dst, load_sem.at[n])
        for n, (src, dst) in enumerate(
            (
                (samples_hbm, samples_ref),
                (q_hbm, q_ref),
                (k_hbm.at[0], keys.at[0]),
                (wq_hbm, wq_ref),
                (wk_hbm, wk_ref),
            )
        )
    ]
    for load in loads:
        load.start()

    barrier = pltpu.get_barrier_semaphore()
    for target in near:
        pl.semaphore_signal(barrier, inc=1, device_id=target, device_id_type=MESH)

    loads[2].wait()
    own = keys[0].astype(jnp.float32)
    blocks = (own[:BLOCK], own[BLOCK:])
    pooled[0, 0] = jnp.concatenate(
        [jnp.max(b, axis=0, keepdims=True) for b in blocks]
        + [jnp.min(b, axis=0, keepdims=True) for b in blocks]
        + [jnp.sum(b, axis=0, keepdims=True) * (1.0 / BLOCK) for b in blocks]
        + [jnp.zeros((2, own.shape[1]), jnp.float32)],
        axis=0,
    )

    loads[0].wait()
    shard = (yl * nz + z) * 2 + c
    local = (samples_ref[...] - shard * (2 * BLOCK)).astype(jnp.float32)
    spread = jnp.concatenate([jnp.broadcast_to(local[h : h + 1], (8, 8)) for h in range(8)], axis=0)
    lanes8 = lax.broadcasted_iota(jnp.int32, (64, 8), 1)
    rows8 = lax.broadcasted_iota(jnp.int32, (64, 8), 0) % 8
    column = jnp.sum(jnp.where(lanes8 == rows8, spread, 0.0), axis=1, keepdims=True)
    tokens = lax.broadcasted_iota(jnp.int32, (8, 2 * BLOCK), 1)
    query_rows, pooled_rows = [], []
    loads[1].wait()
    for h in range(8):
        place = column[8 * h : 8 * h + 8].astype(jnp.int32)
        chosen = jnp.where(tokens == place, 1.0, 0.0)
        block = jnp.where(tokens // BLOCK == place // BLOCK, 1.0, 0.0)
        both = lax.dot_general(
            jnp.concatenate([chosen, block], axis=0).astype(jnp.bfloat16),
            q_ref[h],
            NN,
            preferred_element_type=jnp.float32,
        )
        query_rows.append(both[:8])
        pooled_rows.append(both[8:] * (1.0 / BLOCK))
    queries[0] = jnp.concatenate(query_rows, axis=0).astype(jnp.bfloat16)

    pl.semaphore_wait(barrier, len(near))

    far_places = (far, nz - far)
    group_of = {at: g for g, group in enumerate(groups) for at in group}
    group_of.update({at: len(groups) + n for n, at in enumerate(far_places)})
    waits = [[at for at in group if at not in (0, *far_places)] for group in groups]

    def pass_pool(held, step):
        at = (held + step + nz) % nz
        send(
            pooled.at[0, held, :6],
            pooled.at[0, at, :6],
            pool_send,
            pool_recv.at[group_of[at]],
            along_z(step),
        )

    def pass_query(held, step):
        at = (held + step + nz) % nz
        send(
            queries.at[held],
            queries.at[at],
            query_send,
            query_recv.at[group_of[at]],
            along_z(step),
        )

    for d in reversed(near_z):
        for sign in (1, -1):
            pass_query(0, sign * d)
    for d in reversed(near_z):
        for sign in (1, -1):
            pass_pool(0, sign * d)
    for i in (2, 3, 1):
        send(keys.at[0], keys.at[i], keys_send, keys_recv, in_slice(i))
    pooled_rows = jnp.concatenate(pooled_rows + [jnp.zeros((64, BLOCK), jnp.float32)], axis=0)
    loads[3].wait()
    gate_rows = dot32(pooled_rows, wq_ref[...])
    pooled_columns = pooled_rows.T
    lanes = lax.broadcasted_iota(jnp.int32, (1, 256), 1)
    eye = lax.broadcasted_iota(jnp.int32, (64, 256), 0) == lax.broadcasted_iota(
        jnp.int32, (64, 256), 1
    )
    places = jnp.sum(jnp.where(eye, column, 0.0), axis=0, keepdims=True).astype(jnp.int32)
    places = jnp.where(lanes < 64, places, 2 * BLOCK - 1)

    for pass_on, kept, recv in (
        (pass_query, queries, query_recv),
        (pass_pool, pooled.at[0], pool_recv),
    ):
        for held, steps in zip(far_places, (upper, lower)):
            wait_for(kept.at[held] if kept is queries else kept.at[held, :6], recv.at[group_of[held]])
            for step in steps:
                pass_on(held, step)

    wait_for(keys.at[1:4], keys_recv)
    exponent = math.log2(math.e) / math.sqrt(BLOCK)
    first = lax.broadcasted_iota(jnp.int32, (8, BLOCK), 1) < 64

    def score(slots, waited):
        wait_for(queries.at[: len(waited)], query_recv.at[group_of[waited[0]]])
        rows = jnp.concatenate([queries[at] for at in slots], axis=0)
        tops, sums = [], []
        for i in range(4):
            scores = lax.dot_general(keys[i], rows, NT, preferred_element_type=jnp.float32)
            if i == 0 and slots[0] == 0:
                token = lax.broadcasted_iota(jnp.int32, scores.shape, 0)
                scores = jnp.where(token <= places, scores, LOW)
            for b in range(2):
                block_scores = scores[b * BLOCK : (b + 1) * BLOCK]
                highest_score = jnp.max(block_scores, axis=0, keepdims=True)
                weights = jnp.exp2((block_scores - highest_score) * exponent)
                tops.append(highest_score)
                sums.append(jnp.sum(weights, axis=0, keepdims=True))
        tops = jnp.concatenate(tops, axis=0)
        sums = jnp.concatenate(sums, axis=0)
        for pair in range(len(slots) // 2):
            top = tops[:, pair * BLOCK : (pair + 1) * BLOCK]
            mass = sums[:, pair * BLOCK : (pair + 1) * BLOCK]
            packed[slots[2 * pair]] = jnp.where(first, top, pltpu.roll(mass, 64, 1))
            packed[slots[2 * pair + 1]] = jnp.where(first, pltpu.roll(top, 64, 1), mass)
        for at in slots:
            if at:
                back = nz - at
                send(packed.at[at], returned.at[back], back_send, back_recv, along_z(-at))

    def share_tiles(group, waited):
        wait_for(pooled.at[0, : len(waited), :6], pool_recv.at[group_of[waited[0]]])
        for at in group:
            for i in (2, 3, 1):
                send(
                    pooled.at[0, at, :6], pooled.at[i, at, :6], tile_send, tile_recv, in_slice(i)
                )

    for n, (group, waited) in enumerate(zip(groups, waits)):
        score(group, waited)
        if n < 1:
            share_tiles(group, waited)
    for group, waited in list(zip(groups, waits))[1:]:
        share_tiles(group, waited)
    returned[0] = packed[0]
    loads[4].wait()
    wait_for(pooled.at[1:4, :, :6], tile_recv)

    nb = 8 * nz
    pooled_keys = jnp.concatenate(
        [
            jnp.concatenate([pooled[i, :, 2 * kind + b, :] for kind in range(3)], axis=1)
            for i in range(4)
            for b in range(2)
        ],
        axis=0,
    )
    gate_key = dot32(pooled_keys, wk_ref[...])
    gate_scale = 1.0 / math.sqrt(BLOCK)
    logits = dot32(gate_key, gate_rows, NT) * gate_scale
    order = lax.broadcasted_iota(jnp.int32, (nb, BLOCK), 0)
    lane = lax.broadcasted_iota(jnp.int32, (nb, BLOCK), 1)
    i_of = order // (2 * nz)
    b_of = order // nz % 2
    z_of = (z - order % nz + nz) % nz
    yl_of = (yl + i_of // 2) % 2
    c_of = (c + i_of % 2) % 2
    block_of = ((yl_of * nz + z_of) * 2 + c_of) * 2 + b_of
    own_block = 2 * shard + places[:, :BLOCK] // BLOCK
    allowed = block_of <= own_block
    logit_top = jnp.max(jnp.where(allowed, logits, LOW), axis=0, keepdims=True)
    gate_weights = jnp.where(allowed, jnp.exp(logits - logit_top), 0.0)
    gate_total = jnp.sum(gate_weights, axis=0, keepdims=True)
    log_total = logit_top + jnp.log(gate_total)
    gate = gate_weights / gate_total

    wait_for(returned.at[1:], back_recv)
    pairs = jnp.concatenate([returned[:, r, :] for r in range(8)], axis=0)
    sums = pltpu.roll(pairs, 64, 1)
    row_top = jnp.max(jnp.where(allowed, pairs, LOW), axis=0, keepdims=True)
    masses = jnp.where(allowed, sums * jnp.exp2((pairs - row_top) * exponent), 0.0)
    teacher = masses / jnp.sum(masses, axis=0, keepdims=True)
    losses = log_total - jnp.sum(jnp.where(allowed, teacher * logits, 0.0), axis=0, keepdims=True)
    delta = jnp.where(allowed & (lane < 64), (gate - teacher) * gate_scale, 0.0)

    block_query = dot32(pooled_columns, delta, NT)
    local_sum = dot32(block_query, pooled_keys)
    chunks = nx * ny
    rows = BLOCK // chunks
    for n in range(chunks):
        for kind in range(3):
            part[n, kind] = local_sum[rows * n : rows * (n + 1), BLOCK * kind : BLOCK * (kind + 1)]

    def place_of(n):
        return partner(x, n // (2 * ny), nx) * ny + partner(y, n // 2 % ny, ny)

    for core in (0, 1):

        @pl.when(c == core)
        def share():
            for n in others:
                if n % 2 != core:
                    send(part.at[place_of(n)], from_slice.at[n], sum_send, sum_recv, along_xy(n))

    head_of = lax.broadcasted_iota(jnp.int32, (8, BLOCK), 1) // 8
    head = lax.broadcasted_iota(jnp.int32, (8, BLOCK), 0)
    row_of = lax.broadcasted_iota(jnp.int32, (BLOCK, BLOCK), 0) % 8
    row = lax.broadcasted_iota(jnp.int32, (BLOCK, BLOCK), 1)
    by_head = jnp.where(head_of == head, jnp.broadcast_to(losses, (8, BLOCK)), 0.0)
    loss_ref[...] = dot32(by_head, jnp.where(row_of == row, 1.0, 0.0))[:, :8]
    far_first = sorted(range(1, nz), key=lambda d: -min(d, nz - d))

    @pl.when(c == 1)
    def own():
        wait_for(from_slice.at[1:], sum_recv)
        total = part[place_of(0)]
        for n in range(1, slice_size):
            total = total + from_slice[n]
        slice_sum[...] = total
        for d in far_first:
            send(slice_sum, from_z.at[z], z_send, z_recv, along_z(d))
        from_z[z] = total
        wait_for(from_z.at[1:], z_recv)
        total = from_z[0]
        for i in range(1, nz):
            total = total + from_z[i]
        z_sum[...] = total
        for n in others:
            send(z_sum, total_ref.at[place_of(0)], all_send, all_recv, along_xy(n))
        total_ref[place_of(0)] = total

    wait_for(queries.at[1:], query_send)
    wait_for(pooled.at[0, 1:, :6], pool_send)
    wait_for(keys.at[1:], keys_send)
    wait_for(packed.at[1:], back_send)
    wait_for(pooled.at[1:, :, :6], tile_send)

    @pl.when(c == 0)
    def end_core_0():
        wait_for(part, sum_send)
        wait_for(part, all_recv)

    @pl.when(c == 1)
    def end_core_1():
        wait_for(part.at[1:], sum_send)
        wait_for(from_z.at[1:], z_send)
        wait_for(from_slice.at[1:], all_send)
        wait_for(part.at[1:], all_recv)


def finish(loss_ref, total_ref, wq_ref, wk_ref, row_loss_ref, query_grad_ref, key_grad_ref):
    total = jnp.concatenate(
        [
            jnp.concatenate([total_ref[n, kind] for n in range(total_ref.shape[0])], axis=0)
            for kind in range(3)
        ],
        axis=1,
    )
    query_grad_ref[...] = dot32(total, wk_ref[...])
    key_grad_ref[...] = dot32(total, wq_ref[...], TN)
    row_loss_ref[...] = loss_ref[...]


def body(sizes, queries, key_states, samples, query_gate_weight, key_gate_weight):
    nz, nx, nyh = sizes
    slice_size = 4 * nx * nyh
    chunks = slice_size // 2
    tile = (3, BLOCK // chunks, BLOCK)
    f32, bf16 = jnp.float32, jnp.bfloat16
    dma = pltpu.SemaphoreType.DMA
    vmem = pl.BlockSpec(memory_space=pltpu.VMEM)
    handed = pl.pallas_call(
        functools.partial(kernel, sizes),
        out_shape=(
            pltpu.VMEM((8, 8), f32),
            pltpu.VMEM((chunks, *tile), f32),
            pltpu.VMEM((BLOCK, BLOCK), f32),
            pltpu.VMEM((3 * BLOCK, BLOCK), f32),
        ),
        in_specs=[pl.BlockSpec(memory_space=pl.ANY)] * 5,
        out_specs=(vmem,) * 4,
        scratch_shapes=[
            pltpu.VMEM((8, 2 * BLOCK, BLOCK), bf16),
            pltpu.VMEM((4, 2 * BLOCK, BLOCK), bf16),
            pltpu.VMEM((8, 8), jnp.int32),
            pltpu.VMEM((4, nz, 8, BLOCK), f32),
            pltpu.VMEM((nz, 64, BLOCK), bf16),
            pltpu.VMEM((nz, 8, BLOCK), f32),
            pltpu.VMEM((nz, 8, BLOCK), f32),
            pltpu.VMEM((chunks, *tile), f32),
            pltpu.VMEM((slice_size, *tile), f32),
            pltpu.VMEM(tile, f32),
            pltpu.VMEM((nz, *tile), f32),
            pltpu.VMEM(tile, f32),
            dma((5,)),
            dma,
            dma((len(ROUTES[nz][3]) + 2,)),
            dma,
            dma((len(ROUTES[nz][3]) + 2,)),
        ]
        + [dma] * 12,
        compiler_params=pltpu.CompilerParams(collective_id=0, has_side_effects=True),
    )(queries, key_states, samples, query_gate_weight, key_gate_weight)
    return pl.pallas_call(
        finish,
        out_shape=(
            jax.ShapeDtypeStruct((8, 8), f32),
            jax.ShapeDtypeStruct((BLOCK, BLOCK), f32),
            jax.ShapeDtypeStruct((3 * BLOCK, BLOCK), f32),
        ),
        in_specs=[vmem] * 4,
        out_specs=(vmem,) * 3,
    )(*[pltpu.with_memory_space_constraint(a, pltpu.VMEM) for a in handed])


SEQ = ("yl", "z", "c")
KV = ("x", "yh")


def build(mesh, sizes):
    nz, nx, nyh = sizes
    torus = Mesh(mesh.devices.reshape(2, nz, 2, nx, nyh), (*SEQ, *KV))
    placed = (P(KV, SEQ, None), P(KV, SEQ, None), P(KV, SEQ), P(), P())
    return jax.shard_map(
        functools.partial(body, sizes),
        mesh=torus,
        in_specs=placed,
        out_specs=(P(KV, SEQ), P(), P()),
        check_vma=False,
    )


def solution(mesh):
    return build(mesh, (mesh.shape["seq"] // 4, mesh.shape["kv"] // 2, 2))
```

```python
import functools
import math

import jax
import jax.numpy as jnp
from jax import lax
from jax.experimental import pallas as pl
from jax.experimental.pallas import tpu as pltpu
from jax.sharding import Mesh
from jax.sharding import PartitionSpec as P

BLOCK = 128
MESH = pl.DeviceIdType.MESH
LOW = -1e30
highest = lax.Precision.HIGHEST
NN = (((1,), (0,)), ((), ()))
NT = (((1,), (1,)), ((), ()))
TN = (((0,), (0,)), ((), ()))
ROUTES = {
    4: ((1,), (1,), (), ((0, 1, 2, 3),)),
    8: ((1, 3), (1, -1), (1,), ((0, 1, 7, 3), (5, 4, 2, 6))),
    16: (
        (1, 2, 4),
        (4, 3, 2, 1, -1),
        (-3, -2, -1, 1),
        ((0, 1, 2, 15), (14, 4, 12, 13), (8, 7, 9, 6), (10, 11, 3, 5)),
    ),
}


def dot32(a, b, dims=NN):
    return lax.dot_general(a, b, dims, precision=highest, preferred_element_type=jnp.float32)


def partner(place, apart, size):
    if apart == 0:
        return place
    if size == 2:
        return 1 - place
    return (place + 1 - 2 * (place % 2), (place + 2) % 4, 3 - place)[apart - 1]


def kernel(
    sizes,
    q_hbm,
    k_hbm,
    samples_hbm,
    wq_hbm,
    wk_hbm,
    loss_ref,
    total_ref,
    wq_ref,
    wk_ref,
    q_ref,
    keys,
    samples_ref,
    pooled,
    queries,
    packed,
    returned,
    part,
    from_slice,
    slice_sum,
    from_z,
    z_sum,
    load_sem,
    query_send,
    query_recv,
    pool_send,
    pool_recv,
    keys_send,
    keys_recv,
    tile_send,
    tile_recv,
    back_send,
    back_recv,
    sum_send,
    sum_recv,
    z_send,
    z_recv,
    all_send,
    all_recv,
):
    nz, nx, nyh = sizes
    ny = 2 * nyh
    near_z, upper, lower, groups = ROUTES[nz]
    far = near_z[-1]
    z, yl, c = lax.axis_index("z"), lax.axis_index("yl"), lax.axis_index("c")
    x, yh = lax.axis_index("x"), lax.axis_index("yh")
    y = 2 * yh + yl
    def send(src, dst, send_sem, recv_sem, target):
        copy = pltpu.make_async_remote_copy(
            src_ref=src,
            dst_ref=dst,
            send_sem=send_sem,
            recv_sem=recv_sem,
            device_id=target,
            device_id_type=MESH,
        )
        copy.start()
        return copy

    def wait_for(ref, sem):
        pltpu.make_async_copy(ref, ref, sem).wait()

    def along_z(step):
        return {"z": (z + step + nz) % nz}

    def in_slice(i):
        return {"yl": partner(yl, i // 2, 2), "c": partner(c, i % 2, 2)}

    def along_xy(n):
        other = partner(y, n // 2 % ny, ny)
        return {
            "x": partner(x, n // (2 * ny), nx),
            "yh": other // 2,
            "yl": other % 2,
            "c": partner(c, n % 2, 2),
        }

    slice_size = 2 * nx * ny
    hops = (0, 1, 2, 1)
    others = sorted(
        range(1, slice_size), key=lambda n: -hops[n // (2 * ny)] - hops[n // 2 % ny]
    )
    touched = sorted({*near_z, *map(abs, upper), *map(abs, lower)}, reverse=True)
    near = [along_z(sign * d) for d in touched for sign in (1, -1)]
    near += [along_xy(n) for n in others]
    loads = [
        pltpu.make_async_copy(src, dst, load_sem.at[n])
        for n, (src, dst) in enumerate(
            (
                (samples_hbm, samples_ref),
                (q_hbm, q_ref),
                (k_hbm.at[0], keys.at[0]),
                (wq_hbm, wq_ref),
                (wk_hbm, wk_ref),
            )
        )
    ]
    for load in loads:
        load.start()

    barrier = pltpu.get_barrier_semaphore()
    for target in near:
        pl.semaphore_signal(barrier, inc=1, device_id=target, device_id_type=MESH)

    loads[2].wait()
    own = keys[0].astype(jnp.float32)
    blocks = (own[:BLOCK], own[BLOCK:])
    pooled[0, 0] = jnp.concatenate(
        [jnp.max(b, axis=0, keepdims=True) for b in blocks]
        + [jnp.min(b, axis=0, keepdims=True) for b in blocks]
        + [jnp.sum(b, axis=0, keepdims=True) * (1.0 / BLOCK) for b in blocks]
        + [jnp.zeros((2, own.shape[1]), jnp.float32)],
        axis=0,
    )

    loads[0].wait()
    shard = (yl * nz + z) * 2 + c
    local = (samples_ref[...] - shard * (2 * BLOCK)).astype(jnp.float32)
    spread = jnp.concatenate([jnp.broadcast_to(local[h : h + 1], (8, 8)) for h in range(8)], axis=0)
    lanes8 = lax.broadcasted_iota(jnp.int32, (64, 8), 1)
    rows8 = lax.broadcasted_iota(jnp.int32, (64, 8), 0) % 8
    column = jnp.sum(jnp.where(lanes8 == rows8, spread, 0.0), axis=1, keepdims=True)
    tokens = lax.broadcasted_iota(jnp.int32, (8, 2 * BLOCK), 1)
    query_rows, pooled_rows = [], []
    loads[1].wait()
    for h in range(8):
        place = column[8 * h : 8 * h + 8].astype(jnp.int32)
        chosen = jnp.where(tokens == place, 1.0, 0.0)
        block = jnp.where(tokens // BLOCK == place // BLOCK, 1.0, 0.0)
        both = lax.dot_general(
            jnp.concatenate([chosen, block], axis=0).astype(jnp.bfloat16),
            q_ref[h],
            NN,
            preferred_element_type=jnp.float32,
        )
        query_rows.append(both[:8])
        pooled_rows.append(both[8:] * (1.0 / BLOCK))
    queries[0] = jnp.concatenate(query_rows, axis=0).astype(jnp.bfloat16)

    pl.semaphore_wait(barrier, len(near))

    far_places = (far, nz - far)
    group_of = {at: g for g, group in enumerate(groups) for at in group}
    group_of.update({at: len(groups) + n for n, at in enumerate(far_places)})
    waits = [[at for at in group if at not in (0, *far_places)] for group in groups]

    def pass_pool(held, step):
        at = (held + step + nz) % nz
        send(
            pooled.at[0, held, :6],
            pooled.at[0, at, :6],
            pool_send,
            pool_recv.at[group_of[at]],
            along_z(step),
        )

    def pass_query(held, step):
        at = (held + step + nz) % nz
        send(
            queries.at[held],
            queries.at[at],
            query_send,
            query_recv.at[group_of[at]],
            along_z(step),
        )

    for d in reversed(near_z):
        for sign in (1, -1):
            pass_query(0, sign * d)
    for d in reversed(near_z):
        for sign in (1, -1):
            pass_pool(0, sign * d)
    for i in (2, 3, 1):
        send(keys.at[0], keys.at[i], keys_send, keys_recv, in_slice(i))
    pooled_rows = jnp.concatenate(pooled_rows + [jnp.zeros((64, BLOCK), jnp.float32)], axis=0)
    loads[3].wait()
    gate_rows = dot32(pooled_rows, wq_ref[...])
    pooled_columns = pooled_rows.T
    lanes = lax.broadcasted_iota(jnp.int32, (1, 256), 1)
    eye = lax.broadcasted_iota(jnp.int32, (64, 256), 0) == lax.broadcasted_iota(
        jnp.int32, (64, 256), 1
    )
    places = jnp.sum(jnp.where(eye, column, 0.0), axis=0, keepdims=True).astype(jnp.int32)
    places = jnp.where(lanes < 64, places, 2 * BLOCK - 1)

    for pass_on, kept, recv in (
        (pass_query, queries, query_recv),
        (pass_pool, pooled.at[0], pool_recv),
    ):
        for held, steps in zip(far_places, (upper, lower)):
            wait_for(kept.at[held] if kept is queries else kept.at[held, :6], recv.at[group_of[held]])
            for step in steps:
                pass_on(held, step)

    wait_for(keys.at[1:4], keys_recv)
    exponent = math.log2(math.e) / math.sqrt(BLOCK)
    first = lax.broadcasted_iota(jnp.int32, (8, BLOCK), 1) < 64

    def score(slots, waited):
        wait_for(queries.at[: len(waited)], query_recv.at[group_of[waited[0]]])
        rows = jnp.concatenate([queries[at] for at in slots], axis=0)
        tops, sums = [], []
        for i in range(4):
            scores = lax.dot_general(keys[i], rows, NT, preferred_element_type=jnp.float32)
            if i == 0 and slots[0] == 0:
                token = lax.broadcasted_iota(jnp.int32, scores.shape, 0)
                scores = jnp.where(token <= places, scores, LOW)
            for b in range(2):
                block_scores = scores[b * BLOCK : (b + 1) * BLOCK]
                highest_score = jnp.max(block_scores, axis=0, keepdims=True)
                weights = jnp.exp2((block_scores - highest_score) * exponent)
                tops.append(highest_score)
                sums.append(jnp.sum(weights, axis=0, keepdims=True))
        tops = jnp.concatenate(tops, axis=0)
        sums = jnp.concatenate(sums, axis=0)
        for pair in range(2):
            top = tops[:, pair * BLOCK : (pair + 1) * BLOCK]
            mass = sums[:, pair * BLOCK : (pair + 1) * BLOCK]
            packed[slots[2 * pair]] = jnp.where(first, top, pltpu.roll(mass, 64, 1))
            packed[slots[2 * pair + 1]] = jnp.where(first, pltpu.roll(top, 64, 1), mass)
        for at in slots:
            if at:
                back = nz - at
                send(packed.at[at], returned.at[back], back_send, back_recv, along_z(-at))

    def share_tiles(group, waited):
        wait_for(pooled.at[0, : len(waited), :6], pool_recv.at[group_of[waited[0]]])
        for at in group:
            for i in (2, 3, 1):
                send(
                    pooled.at[0, at, :6], pooled.at[i, at, :6], tile_send, tile_recv, in_slice(i)
                )

    for n, (group, waited) in enumerate(zip(groups, waits)):
        score(group, waited)
        if n < 1:
            share_tiles(group, waited)
    for group, waited in list(zip(groups, waits))[1:]:
        share_tiles(group, waited)
    returned[0] = packed[0]
    loads[4].wait()
    wait_for(pooled.at[1:4, :, :6], tile_recv)

    nb = 8 * nz
    pooled_keys = jnp.concatenate(
        [
            jnp.concatenate([pooled[i, :, 2 * kind + b, :] for kind in range(3)], axis=1)
            for i in range(4)
            for b in range(2)
        ],
        axis=0,
    )
    gate_key = dot32(pooled_keys, wk_ref[...])
    gate_scale = 1.0 / math.sqrt(BLOCK)
    logits = dot32(gate_key, gate_rows, NT) * gate_scale
    order = lax.broadcasted_iota(jnp.int32, (nb, BLOCK), 0)
    lane = lax.broadcasted_iota(jnp.int32, (nb, BLOCK), 1)
    i_of = order // (2 * nz)
    b_of = order // nz % 2
    z_of = (z - order % nz + nz) % nz
    yl_of = (yl + i_of // 2) % 2
    c_of = (c + i_of % 2) % 2
    block_of = ((yl_of * nz + z_of) * 2 + c_of) * 2 + b_of
    own_block = 2 * shard + places[:, :BLOCK] // BLOCK
    allowed = block_of <= own_block
    logit_top = jnp.max(jnp.where(allowed, logits, LOW), axis=0, keepdims=True)
    gate_weights = jnp.where(allowed, jnp.exp(logits - logit_top), 0.0)
    gate_total = jnp.sum(gate_weights, axis=0, keepdims=True)
    log_total = logit_top + jnp.log(gate_total)
    gate = gate_weights / gate_total

    wait_for(returned.at[1:], back_recv)
    pairs = jnp.concatenate([returned[:, r, :] for r in range(8)], axis=0)
    sums = pltpu.roll(pairs, 64, 1)
    row_top = jnp.max(jnp.where(allowed, pairs, LOW), axis=0, keepdims=True)
    masses = jnp.where(allowed, sums * jnp.exp2((pairs - row_top) * exponent), 0.0)
    teacher = masses / jnp.sum(masses, axis=0, keepdims=True)
    losses = log_total - jnp.sum(jnp.where(allowed, teacher * logits, 0.0), axis=0, keepdims=True)
    delta = jnp.where(allowed & (lane < 64), (gate - teacher) * gate_scale, 0.0)

    block_query = dot32(pooled_columns, delta, NT)
    local_sum = dot32(block_query, pooled_keys)
    chunks = nx * ny
    rows = BLOCK // chunks
    for n in range(chunks):
        for kind in range(3):
            part[n, kind] = local_sum[rows * n : rows * (n + 1), BLOCK * kind : BLOCK * (kind + 1)]

    def place_of(n):
        return partner(x, n // (2 * ny), nx) * ny + partner(y, n // 2 % ny, ny)

    for core in (0, 1):

        @pl.when(c == core)
        def share():
            for n in others:
                if n % 2 != core:
                    send(part.at[place_of(n)], from_slice.at[n], sum_send, sum_recv, along_xy(n))

    head_of = lax.broadcasted_iota(jnp.int32, (8, BLOCK), 1) // 8
    head = lax.broadcasted_iota(jnp.int32, (8, BLOCK), 0)
    row_of = lax.broadcasted_iota(jnp.int32, (BLOCK, BLOCK), 0) % 8
    row = lax.broadcasted_iota(jnp.int32, (BLOCK, BLOCK), 1)
    by_head = jnp.where(head_of == head, jnp.broadcast_to(losses, (8, BLOCK)), 0.0)
    loss_ref[...] = dot32(by_head, jnp.where(row_of == row, 1.0, 0.0))[:, :8]
    far_first = sorted(range(1, nz), key=lambda d: -min(d, nz - d))

    @pl.when(c == 1)
    def own():
        wait_for(from_slice.at[1:], sum_recv)
        total = part[place_of(0)]
        for n in range(1, slice_size):
            total = total + from_slice[n]
        slice_sum[...] = total
        for d in far_first:
            send(slice_sum, from_z.at[z], z_send, z_recv, along_z(d))
        from_z[z] = total
        wait_for(from_z.at[1:], z_recv)
        total = from_z[0]
        for i in range(1, nz):
            total = total + from_z[i]
        z_sum[...] = total
        for n in others:
            send(z_sum, total_ref.at[place_of(0)], all_send, all_recv, along_xy(n))
        total_ref[place_of(0)] = total

    wait_for(queries.at[1:], query_send)
    wait_for(pooled.at[0, 1:, :6], pool_send)
    wait_for(keys.at[1:], keys_send)
    wait_for(packed.at[1:], back_send)
    wait_for(pooled.at[1:, :, :6], tile_send)

    @pl.when(c == 0)
    def end_core_0():
        wait_for(part, sum_send)
        wait_for(part, all_recv)

    @pl.when(c == 1)
    def end_core_1():
        wait_for(part.at[1:], sum_send)
        wait_for(from_z.at[1:], z_send)
        wait_for(from_slice.at[1:], all_send)
        wait_for(part.at[1:], all_recv)


def finish(loss_ref, total_ref, wq_ref, wk_ref, row_loss_ref, query_grad_ref, key_grad_ref):
    total = jnp.concatenate(
        [
            jnp.concatenate([total_ref[n, kind] for n in range(total_ref.shape[0])], axis=0)
            for kind in range(3)
        ],
        axis=1,
    )
    query_grad_ref[...] = dot32(total, wk_ref[...])
    key_grad_ref[...] = dot32(total, wq_ref[...], TN)
    row_loss_ref[...] = loss_ref[...]


def body(sizes, queries, key_states, samples, query_gate_weight, key_gate_weight):
    nz, nx, nyh = sizes
    slice_size = 4 * nx * nyh
    chunks = slice_size // 2
    tile = (3, BLOCK // chunks, BLOCK)
    f32, bf16 = jnp.float32, jnp.bfloat16
    dma = pltpu.SemaphoreType.DMA
    vmem = pl.BlockSpec(memory_space=pltpu.VMEM)
    handed = pl.pallas_call(
        functools.partial(kernel, sizes),
        out_shape=(
            pltpu.VMEM((8, 8), f32),
            pltpu.VMEM((chunks, *tile), f32),
            pltpu.VMEM((BLOCK, BLOCK), f32),
            pltpu.VMEM((3 * BLOCK, BLOCK), f32),
        ),
        in_specs=[pl.BlockSpec(memory_space=pl.ANY)] * 5,
        out_specs=(vmem,) * 4,
        scratch_shapes=[
            pltpu.VMEM((8, 2 * BLOCK, BLOCK), bf16),
            pltpu.VMEM((4, 2 * BLOCK, BLOCK), bf16),
            pltpu.VMEM((8, 8), jnp.int32),
            pltpu.VMEM((4, nz, 8, BLOCK), f32),
            pltpu.VMEM((nz, 64, BLOCK), bf16),
            pltpu.VMEM((nz, 8, BLOCK), f32),
            pltpu.VMEM((nz, 8, BLOCK), f32),
            pltpu.VMEM((chunks, *tile), f32),
            pltpu.VMEM((slice_size, *tile), f32),
            pltpu.VMEM(tile, f32),
            pltpu.VMEM((nz, *tile), f32),
            pltpu.VMEM(tile, f32),
            dma((5,)),
            dma,
            dma((len(ROUTES[nz][3]) + 2,)),
            dma,
            dma((len(ROUTES[nz][3]) + 2,)),
        ]
        + [dma] * 12,
        compiler_params=pltpu.CompilerParams(collective_id=0, has_side_effects=True),
    )(queries, key_states, samples, query_gate_weight, key_gate_weight)
    return pl.pallas_call(
        finish,
        out_shape=(
            jax.ShapeDtypeStruct((8, 8), f32),
            jax.ShapeDtypeStruct((BLOCK, BLOCK), f32),
            jax.ShapeDtypeStruct((3 * BLOCK, BLOCK), f32),
        ),
        in_specs=[vmem] * 4,
        out_specs=(vmem,) * 3,
    )(*[pltpu.with_memory_space_constraint(a, pltpu.VMEM) for a in handed])


SEQ = ("yl", "z", "c")
KV = ("x", "yh")


def build(mesh, sizes):
    nz, nx, nyh = sizes
    torus = Mesh(mesh.devices.reshape(2, nz, 2, nx, nyh), (*SEQ, *KV))
    placed = (P(KV, SEQ, None), P(KV, SEQ, None), P(KV, SEQ), P(), P())
    return jax.shard_map(
        functools.partial(body, sizes),
        mesh=torus,
        in_specs=placed,
        out_specs=(P(KV, SEQ), P(), P()),
        check_vma=False,
    )


def solution(mesh):
    return build(mesh, (mesh.shape["seq"] // 4, mesh.shape["kv"] // 2, 2))
```
